32 devices in a mesh: dp: 2 (over x), ctx: 16 (over z, y, core).
Axes of the slice: x: 2, y: 2, z: 4, core: 2. Of those that a mesh axis runs over, the one named last changes fastest.
Arguments:
- token_ids: int32 [2, 2048], P('dp', 'ctx'), may hold values from 0 to 7
- queries: bfloat16 [2, 2048, 4096], P('dp', 'ctx'), may hold values from -6 to 6
- gated_values: bfloat16 [2, 2048, 4096], P('dp', 'ctx'), may hold values from -6 to 6
- out_grad: bfloat16 [2, 2048, 4096], P('dp', 'ctx'), may hold values from -6 to 6
- filters: bfloat16 [4096, 128], P('ctx'), may hold values from -0.5 to 0.5
Outputs:
- value_grad: bfloat16 [2, 2048, 4096], P('dp', 'ctx')
- filter_grad: float32 [4096, 128], P('ctx')
The draws below stay inside these ranges and needn't reach their ends.
Inputs may be any that keep to these rules, and one draw needn't show every extreme that they name: `token_ids`: ids 0 to 3 are upper-case bases, 4 to 7 lower-case bases.
All inputs are finite; a program needn't handle non-finite values.
Results may differ from the reference program's by a relative error of at most 0.0049.
Values may be sent and summed in bfloat16 or wider, within the bound.
No kernel may reach another device: no remote copies, remote signals or barrier semaphores. Data moves between devices by JAX's collectives and lax.ppermute only.
A program may use at most 64 MiB of HBM per device.

```python
import jax
import jax.numpy as jnp
from jax import lax

D = 4096
TAPS = 128
LENGTH = 2048
SEQS = 2
ALLTOK = 4096


def plant(values, stream_key, least, top_value):
    place = [jax.random.randint(jax.random.fold_in(stream_key, axis), (), 0, length) for axis, length in enumerate(values.shape)]
    widest = values.shape.index(max(values.shape))
    beside = place[:widest] + [(place[widest] + 1) % values.shape[widest]] + place[widest + 1:]
    return values.at[tuple(place)].set(least).at[tuple(beside)].set(top_value)


def levels(own_key, extent, pieces, least, high):
    level, own = 1.0, jax.random.fold_in(own_key, 6)
    for axis_at, blocks in pieces:
        steps = jnp.exp(jax.random.uniform(jax.random.fold_in(own, axis_at), (blocks,), jnp.float32, least / len(pieces), high / len(pieces)))
        level = level * jnp.repeat(steps, extent[axis_at] // blocks).reshape([-1 if axis == axis_at else 1 for axis in range(len(extent))])
    return level


def noise(stream_key, dims, width, reach, cuts=(), held_as=jnp.bfloat16):
    values = width * jax.random.normal(stream_key, dims, jnp.float32)
    if cuts:
        values = values * levels(stream_key, dims, cuts, -0.22, 0.18)
    return jnp.clip(values, -reach, reach).astype(held_as)


def setup_inputs(seed: int = 0) -> dict:
    streams_of = jax.random.split(jax.random.key(seed), 6)
    token_ids = plant(jax.random.randint(streams_of[0], (SEQS, LENGTH), 0, 8), jax.random.fold_in(streams_of[0], 1), 0, 7).astype(jnp.int32)
    queries = noise(streams_of[1], (SEQS, LENGTH, D), 1.0, 6.0, ((0, 2), (1, 16)))
    gated_values = noise(streams_of[2], (SEQS, LENGTH, D), 1.0, 6.0, ((0, 2), (1, 16)))
    out_grad = noise(streams_of[3], (SEQS, LENGTH, D), 1.0, 6.0, ((0, 2), (1, 16)))
    filters = noise(streams_of[4], (D, TAPS), TAPS ** -0.5, 0.5, ((0, 16),))
    return dict(token_ids=token_ids, queries=queries, gated_values=gated_values, out_grad=out_grad, filters=filters)


def reference(token_ids, queries, gated_values, out_grad, filters):
    weight = jnp.where(token_ids < 4, 1.0, 0.1).astype(jnp.float32)
    product = weight[:, :, None] * out_grad.astype(jnp.float32) * queries.astype(jnp.float32)
    cotangent = lax.optimization_barrier(product.astype(jnp.bfloat16)).astype(jnp.float32)
    span = 2 * LENGTH
    filter_freq = jnp.fft.rfft(filters.T.astype(jnp.float32), n=span, axis=0)

    def per_sequence(pair):
        cot_seq, val_seq = pair
        cot_freq = jnp.fft.rfft(cot_seq, n=span, axis=0)
        val_freq = jnp.fft.rfft(val_seq.astype(jnp.float32), n=span, axis=0)
        grad_seq = jnp.fft.irfft(cot_freq * jnp.conj(filter_freq), n=span, axis=0)[:LENGTH]
        tap_seq = jnp.fft.irfft(cot_freq * jnp.conj(val_freq), n=span, axis=0)[:TAPS]
        return grad_seq.astype(jnp.float32).astype(jnp.bfloat16), tap_seq.astype(jnp.float32)

    value_grad, tap_terms = lax.map(per_sequence, (cotangent, gated_values))
    filter_grad = (jnp.sum(tap_terms, axis=0).T * (ALLTOK ** -0.5)).astype(jnp.float32)
    return value_grad, filter_grad
```

```python
import functools

import jax
import jax.numpy as jnp
import numpy as np
from jax import lax
from jax.experimental import pallas as pl
from jax.experimental.pallas import tpu as pltpu
from jax.sharding import PartitionSpec as P

BF16 = jnp.bfloat16
F32 = jnp.float32
AXES = ("dp", "ctx")
LANES = 128


def split_bf16(matrix):
    high = matrix.astype(BF16)
    low = (matrix - high.astype(np.float64)).astype(BF16)
    return np.asarray(high), np.asarray(low)


@functools.lru_cache(None)
def transforms(positions, taps):
    window = positions + taps
    half = window // 2
    angle = 2.0 * np.pi * np.outer(np.arange(half) + 0.5, np.arange(window)) / window
    forward = np.concatenate([np.cos(angle), np.sin(angle)], axis=0)
    high, low = split_bf16(forward)
    of_window = np.concatenate([high, low], axis=0)
    of_values = np.concatenate([high[:, :positions], low[:, :positions]], axis=1)
    of_taps = np.concatenate([high[:, :taps], low[:, :taps]], axis=1)
    inverse = forward.T / half
    inv_high, inv_low = split_bf16(inverse)
    to_taps = np.concatenate([inv_high[:taps], inv_low[:taps]], axis=0)
    to_positions = np.concatenate([inv_high[:positions], inv_low[:positions]], axis=0)
    return of_window, of_values, of_taps, to_taps, to_positions


def mul(a, b):
    return jnp.dot(a, b, preferred_element_type=F32)


def spectrum_of_window(matrix, own, after):
    both = mul(matrix, jnp.concatenate([own, after], axis=0))
    rows = both.shape[0] // 2
    return both[:rows] + both[rows:]


def correlate(x, y, inverse):
    half = x.shape[0] // 2
    a, b, c, d = x[:half], x[half:], y[:half], y[half:]
    product = jnp.concatenate([a * c + b * d, b * c - a * d], axis=0)
    high = product.astype(BF16)
    low = (product - high.astype(F32)).astype(BF16)
    rows = inverse.shape[0] // 2
    both = mul(inverse, high)
    return both[:rows] + both[rows:] + mul(inverse[:rows], low)


def cotangent_kernel(ids_ref, q_ref, g_ref, o_ref):
    positions = ids_ref.shape[1]
    weight = jnp.where(ids_ref[...] < 4, 1.0, 0.1).astype(F32)
    weight = jnp.broadcast_to(weight, (LANES, positions)).T
    for at in range(0, o_ref.shape[1], LANES):
        cols = pl.ds(at, LANES)
        o_ref[:, cols] = (
            weight * g_ref[:, cols].astype(F32) * q_ref[:, cols].astype(F32)
        ).astype(BF16)


def cotangent_of(token_ids, queries, out_grad, tile):
    positions, channels = queries.shape
    block = pl.BlockSpec((positions, tile), lambda i: (0, i))
    return pl.pallas_call(
        cotangent_kernel,
        grid=(channels // tile,),
        in_specs=[pl.BlockSpec((1, positions), lambda i: (0, 0)), block, block],
        out_specs=block,
        out_shape=jax.ShapeDtypeStruct((positions, channels), BF16),
        cost_estimate=pl.CostEstimate(
            flops=2 * positions * channels,
            bytes_accessed=6 * positions * channels,
            transcendentals=0,
        ),
        name="cotangent",
    )(token_ids, queries, out_grad)


def tap_grad_tile(cot_ref, after_ref, val_ref, wx_ref, wv_ref, wi_ref):
    x = spectrum_of_window(wx_ref[...], cot_ref[...], after_ref[...])
    values = val_ref[...]
    y = mul(wv_ref[...], jnp.concatenate([values, values], axis=0))
    return correlate(x, y, wi_ref[...])


def tap_grad_slots_kernel(
    me_ref, cot_ref, after_ref, val_ref, wx_ref, wv_ref, wi_ref, keep_ref, send_ref, tmp_ref
):
    out = tap_grad_tile(cot_ref, after_ref, val_ref, wx_ref, wv_ref, wi_ref)
    low = me_ref[0] % 4
    for block in range(4):
        tmp_ref[block ^ low] = out[:, block * LANES : (block + 1) * LANES]
    for half in range(2):
        keep_ref[half, 0, 0] = tmp_ref[half]
        send_ref[half, 0, 0] = tmp_ref[2 + half].astype(BF16)


def tap_grad_slots(me, cotangent, after, values, taps):
    positions, channels = cotangent.shape
    tile = 4 * LANES
    tiles = channels // tile
    wx, wv, _, wi, _ = transforms(positions, taps)
    data = pl.BlockSpec((positions, tile), lambda t, me: (0, t ^ (me[0] // 4)))
    whole = lambda w: pl.BlockSpec(w.shape, lambda t, me: (0, 0))
    shape = (2, 2, tiles // 2, taps, LANES)
    slot = pl.BlockSpec((2, 1, 1, taps, LANES), lambda t, me: (0, t % 2, t // 2, 0, 0))
    return pl.pallas_call(
        tap_grad_slots_kernel,
        grid_spec=pltpu.PrefetchScalarGridSpec(
            num_scalar_prefetch=1,
            grid=(tiles,),
            in_specs=[data, data, data, whole(wx), whole(wv), whole(wi)],
            out_specs=[slot, slot],
            scratch_shapes=[pltpu.VMEM((4, taps, LANES), F32)],
        ),
        out_shape=[jax.ShapeDtypeStruct(shape, F32), jax.ShapeDtypeStruct(shape, BF16)],
        cost_estimate=pl.CostEstimate(
            flops=2 * 9 * 128 * 256 * channels,
            bytes_accessed=9 * positions * channels,
            transcendentals=0,
        ),
        name="tap_grad_slots",
    )(me, cotangent, after, values, wx, wv, wi)


def tap_grad_plain_kernel(cot_ref, after_ref, val_ref, wx_ref, wv_ref, wi_ref, o_ref):
    o_ref[...] = tap_grad_tile(cot_ref, after_ref, val_ref, wx_ref, wv_ref, wi_ref)


def tap_grad_plain(cotangent, after, values, taps, tile):
    positions, channels = cotangent.shape
    wx, wv, _, wi, _ = transforms(positions, taps)
    data = pl.BlockSpec((positions, tile), lambda t: (0, t))
    whole = lambda w: pl.BlockSpec(w.shape, lambda t: (0, 0))
    return pl.pallas_call(
        tap_grad_plain_kernel,
        grid=(channels // tile,),
        in_specs=[data, data, data, whole(wx), whole(wv), whole(wi)],
        out_specs=pl.BlockSpec((taps, tile), lambda t: (0, t)),
        out_shape=jax.ShapeDtypeStruct((taps, channels), F32),
        name="tap_grad_plain",
    )(cotangent, after, values, wx, wv, wi)


def value_grad_tile(cot_ref, after_ref, filters, wx_ref, wf_ref, wi_ref):
    x = spectrum_of_window(wx_ref[...], cot_ref[...], after_ref[...])
    y = lax.dot_general(
        wf_ref[...],
        jnp.concatenate([filters, filters], axis=1),
        (((1,), (1,)), ((), ())),
        preferred_element_type=F32,
    )
    return correlate(x, y, wi_ref[...]).astype(BF16)


def value_grad_slots_kernel(
    me_ref, cot_ref, after_ref, mine_ref, other_ref, wx_ref, wf_ref, wi_ref, o_ref
):
    even = (me_ref[0] // 2) % 2 == 0
    mine, other = mine_ref[0, 0], other_ref[0, 0]
    filters = jnp.concatenate(
        [jnp.where(even, mine, other), jnp.where(even, other, mine)], axis=0
    )
    o_ref[...] = value_grad_tile(cot_ref, after_ref, filters, wx_ref, wf_ref, wi_ref)


def value_grad_slots(me, cotangent, after, mine, other):
    positions, channels = cotangent.shape
    _, _, shard, taps = mine.shape
    tile = 2 * shard
    tiles = channels // tile
    wx, _, wf, _, wi = transforms(positions, taps)
    data = pl.BlockSpec((positions, tile), lambda t, me: (0, t ^ (me[0] // 4)))
    part = pl.BlockSpec((1, 1, shard, taps), lambda t, me: (t % 2, t // 2, 0, 0))
    whole = lambda w: pl.BlockSpec(w.shape, lambda t, me: (0, 0))
    return pl.pallas_call(
        value_grad_slots_kernel,
        grid_spec=pltpu.PrefetchScalarGridSpec(
            num_scalar_prefetch=1,
            grid=(tiles,),
            in_specs=[data, data, part, part, whole(wx), whole(wf), whole(wi)],
            out_specs=data,
        ),
        out_shape=jax.ShapeDtypeStruct((positions, channels), BF16),
        cost_estimate=pl.CostEstimate(
            flops=2 * 9 * 128 * 256 * channels,
            bytes_accessed=8 * positions * channels,
            transcendentals=0,
        ),
        name="value_grad_slots",
    )(me, cotangent, after, mine, other, wx, wf, wi)


def value_grad_plain_kernel(cot_ref, after_ref, f_ref, wx_ref, wf_ref, wi_ref, o_ref):
    o_ref[...] = value_grad_tile(cot_ref, after_ref, f_ref[...], wx_ref, wf_ref, wi_ref)


def value_grad_plain(cotangent, after, filters, tile):
    positions, channels = cotangent.shape
    taps = filters.shape[1]
    wx, _, wf, _, wi = transforms(positions, taps)
    data = pl.BlockSpec((positions, tile), lambda t: (0, t))
    whole = lambda w: pl.BlockSpec(w.shape, lambda t: (0, 0))
    return pl.pallas_call(
        value_grad_plain_kernel,
        grid=(channels // tile,),
        in_specs=[data, data, pl.BlockSpec((tile, taps), lambda t: (t, 0)), whole(wx), whole(wf), whole(wi)],
        out_specs=data,
        out_shape=jax.ShapeDtypeStruct((positions, channels), BF16),
        name="value_grad_plain",
    )(cotangent, after, filters, wx, wf, wi)


def body(token_ids, queries, gated_values, out_grad, filters):
    queries, gated_values, out_grad = queries[0], gated_values[0], out_grad[0]
    positions, channels = queries.shape
    shard, taps = filters.shape
    seqs, parts = lax.axis_size("dp"), lax.axis_size("ctx")
    factor = float(seqs * parts * positions) ** -0.5

    cotangent = cotangent_of(token_ids, queries, out_grad, 1024)
    after = lax.ppermute(cotangent, "ctx", [(i, i - 1) for i in range(1, parts)])

    staged = seqs == 2 and parts >= 4 and parts & (parts - 1) == 0 and shard == 2 * LANES
    if not staged:
        all_filters = lax.all_gather(filters, "ctx", axis=0, tiled=True)
        value_grad = value_grad_plain(cotangent, after, all_filters, 512)
        share = tap_grad_plain(cotangent, after, gated_values, taps, 512)
        share = lax.psum_scatter(share.T * factor, "ctx", scatter_dimension=0, tiled=True)
        return value_grad[None], lax.psum(share, "dp")

    devices = seqs * parts
    rank = lax.axis_index("dp")
    place = lax.axis_index("ctx")
    me = (place * 2 + rank).astype(jnp.int32).reshape(1)

    def swap(x, bits):
        return lax.ppermute(x, AXES, [(i, i ^ bits) for i in range(devices)])

    line = jnp.stack([filters] + [swap(filters, 4 * k) for k in range(1, parts // 4)])
    mine = jnp.stack([line, swap(line, 2)])
    other = swap(mine, 1)

    keep, send = tap_grad_slots(me, cotangent, after, gated_values, taps)
    keep = keep + swap(send, 1).astype(F32)
    total = keep[0, 0]
    for x, y in ((1, 0), (0, 1), (1, 1)):
        total = total + swap(keep[x, y].astype(BF16), parts * x + 2 * y).astype(F32)
    block = total[0]
    for k in range(1, parts // 4):
        block = block + swap(total[k].astype(BF16), 4 * k).astype(F32)
    block = block * factor
    across = swap(block, parts)
    first = jnp.where(rank == 0, block, across)
    second = jnp.where(rank == 0, across, block)
    filter_grad = jnp.concatenate([first, second], axis=1).T

    value_grad = value_grad_slots(me, cotangent, after, mine, other)
    return value_grad[None], filter_grad


def solution(mesh):
    return jax.shard_map(
        body,
        mesh=mesh,
        in_specs=(
            P("dp", "ctx"),
            P("dp", "ctx", None),
            P("dp", "ctx", None),
            P("dp", "ctx", None),
            P("ctx", None),
        ),
        out_specs=(P("dp", "ctx", None), P("ctx", None)),
        check_vma=False,
    )
```

```python
import functools

import jax
import jax.numpy as jnp
import numpy as np
from jax import lax
from jax.experimental import pallas as pl
from jax.experimental.pallas import tpu as pltpu
from jax.sharding import PartitionSpec as P


BF16 = jnp.bfloat16
F32 = jnp.float32
AXES = ("dp", "ctx")
LANES = 128


def split_bf16(matrix):
    high = matrix.astype(BF16)
    low = (matrix - high.astype(np.float64)).astype(BF16)
    return np.asarray(high), np.asarray(low)


@functools.lru_cache(None)
def transforms(positions, taps):
    window = positions + taps
    half = window // 2
    angle = 2.0 * np.pi * np.outer(np.arange(half) + 0.5, np.arange(window)) / window
    forward = np.concatenate([np.cos(angle), np.sin(angle)], axis=0)
    high, low = split_bf16(forward)
    of_window = np.concatenate([high, low], axis=0)
    of_values = np.concatenate([high[:, :positions], low[:, :positions]], axis=1)
    of_taps = np.concatenate([high[:, :taps], low[:, :taps]], axis=1)
    inverse = forward.T / half
    inv_high, inv_low = split_bf16(inverse)
    to_taps = np.concatenate([inv_high[:taps], inv_low[:taps]], axis=0)
    to_positions = np.concatenate([inv_high[:positions], inv_low[:positions]], axis=0)
    return of_window, of_values, of_taps, to_taps, to_positions


def mul(a, b):
    return jnp.dot(a, b, preferred_element_type=F32)


def spectrum_of_window(matrix, own, after):
    both = mul(matrix, jnp.concatenate([own, after], axis=0))
    rows = both.shape[0] // 2
    return both[:rows] + both[rows:]


def correlate(x, y, inverse):
    half = x.shape[0] // 2
    a, b, c, d = x[:half], x[half:], y[:half], y[half:]
    product = jnp.concatenate([a * c + b * d, b * c - a * d], axis=0)
    high = product.astype(BF16)
    low = (product - high.astype(F32)).astype(BF16)
    rows = inverse.shape[0] // 2
    both = mul(inverse, high)
    return both[:rows] + both[rows:] + mul(inverse[:rows], low)


VMEM_SPEC = pl.BlockSpec(memory_space=pltpu.VMEM)
SMEM_SPEC = pl.BlockSpec(memory_space=pltpu.SMEM)
HBM_SPEC = pl.BlockSpec(memory_space=pltpu.HBM)


def params(mib):
    return pltpu.CompilerParams(vmem_limit_bytes=mib << 20)


def cost(flops, nbytes):
    return pl.CostEstimate(flops=flops, bytes_accessed=nbytes, transcendentals=0)


def cotangent_kernel(ids_ref, q_hbm, g_hbm, *refs):
    *outs, q_ref, g_ref, sems = refs
    width = outs[0].shape[1]
    copies = []
    for i in range(len(outs)):
        cols = pl.ds(i * width, width)
        copies.append(
            [
                pltpu.make_async_copy(src.at[:, cols], dst.at[:, cols], sems.at[n, i])
                for n, (src, dst) in enumerate(((q_hbm, q_ref), (g_hbm, g_ref)))
            ]
        )
        for copy in copies[-1]:
            copy.start()
    positions = ids_ref.shape[1]
    weight = jnp.where(ids_ref[...] < 4, 1.0, 0.1).astype(F32)
    weight = jnp.broadcast_to(weight, (LANES, positions)).T
    for i, out in enumerate(outs):
        for copy in copies[i]:
            copy.wait()
        for at in range(0, width, LANES):
            cols = pl.ds(i * width + at, LANES)
            out[:, at : at + LANES] = (
                weight * g_ref[:, cols].astype(F32) * q_ref[:, cols].astype(F32)
            ).astype(BF16)


def cotangent_of(token_ids, queries, out_grad, pieces):
    positions, channels = queries.shape
    piece = jax.ShapeDtypeStruct((positions, channels // pieces), BF16)
    return pl.pallas_call(
        cotangent_kernel,
        in_specs=[VMEM_SPEC, HBM_SPEC, HBM_SPEC],
        out_specs=[VMEM_SPEC] * pieces,
        out_shape=[piece] * pieces,
        scratch_shapes=[pltpu.VMEM((positions, channels), BF16)] * 2
        + [pltpu.SemaphoreType.DMA((2, pieces))],
        compiler_params=params(8),
        cost_estimate=cost(2 * positions * channels, 6 * positions * channels),
        name="cotangent",
    )(token_ids, *(pltpu.with_memory_space_constraint(x, pltpu.HBM) for x in (queries, out_grad)))


def tap_grad_tile(cot_ref, after_ref, val_ref, wx_ref, wv_ref, wi_ref):
    x = spectrum_of_window(wx_ref[...], cot_ref[...], after_ref[...])
    values = val_ref[...]
    y = mul(wv_ref[...], jnp.concatenate([values, values], axis=0))
    return correlate(x, y, wi_ref[...])


def tap_grad_slots_kernel(
    first, me_ref, cot_ref, after_ref, val_ref, wx_ref, wv_ref, wi_ref, keep_ref, send_ref, tmp_ref
):
    width = cot_ref.shape[1]
    x = spectrum_of_window(wx_ref[...], cot_ref[...], after_ref[...])
    values = val_ref[:, first * width : (first + 1) * width]
    y = mul(wv_ref[...], jnp.concatenate([values, values], axis=0))
    out = correlate(x, y, wi_ref[...])
    low, row = me_ref[0] % 4, me_ref[0] // 4 % 2
    for tile in range(width // (4 * LANES)):
        for block in range(4):
            at = (tile * 4 + block) * LANES
            tmp_ref[tile, block ^ low] = out[:, at : at + LANES]
        for half in range(2):
            keep_ref[half, tile % 2 ^ row, tile // 2] = tmp_ref[tile, half]
            send_ref[half, tile % 2 ^ row, tile // 2] = tmp_ref[tile, 2 + half].astype(BF16)


def tap_grad_slots(me, cotangent, after, values, first, taps):
    positions, width = cotangent.shape
    wx, wv, _, wi, _ = transforms(positions, taps)
    tiles = width // (4 * LANES)
    shape = (2, 2, tiles // 2, taps, LANES)
    return pl.pallas_call(
        functools.partial(tap_grad_slots_kernel, first),
        in_specs=[SMEM_SPEC] + [VMEM_SPEC] * 6,
        out_specs=[VMEM_SPEC, VMEM_SPEC],
        out_shape=[jax.ShapeDtypeStruct(shape, F32), jax.ShapeDtypeStruct(shape, BF16)],
        scratch_shapes=[pltpu.VMEM((tiles, 4, taps, LANES), F32)],
        compiler_params=params(24),
        cost_estimate=cost(2 * 9 * 128 * 256 * width, 9 * positions * width),
        name="tap_grad_slots",
    )(me, cotangent, after, values, wx, wv, wi)


def spread_kernel(keep_ref, got_ref, mine_ref, *out_refs):
    mine_ref[...] = keep_ref[0, 0] + got_ref[0, 0].astype(F32)
    for (x, y), out_ref in zip(((1, 0), (0, 1), (1, 1)), out_refs):
        out_ref[...] = (keep_ref[x, y] + got_ref[x, y].astype(F32)).astype(BF16)


def spread(keep, got):
    block = keep.shape[2:]
    return pl.pallas_call(
        spread_kernel,
        in_specs=[VMEM_SPEC] * 2,
        out_specs=[VMEM_SPEC] * 4,
        out_shape=[jax.ShapeDtypeStruct(block, F32)] + [jax.ShapeDtypeStruct(block, BF16)] * 3,
        compiler_params=params(8),
        cost_estimate=cost(keep.size, 8 * keep.size),
        name="spread",
    )(keep, got)


def line_kernel(pieces, me_ref, *refs):
    ins, (mine_ref, *send_refs) = refs[: 4 * pieces], refs[4 * pieces : -1]
    sum_ref = refs[-1]
    depth = ins[0].shape[0]
    for piece in range(pieces):
        own, *got = ins[4 * piece : 4 * piece + 4]
        for z in range(depth):
            total = own[z]
            for ref in got:
                total = total + ref[z].astype(F32)
            sum_ref[piece * depth + z] = total
    at = me_ref[0] // 8
    mine_ref[...] = sum_ref[at]
    for k, send_ref in enumerate(send_refs, 1):
        send_ref[...] = sum_ref[at ^ k].astype(BF16)


def along_line(me, pieces):
    depth, taps, lanes = pieces[0][0].shape
    count = len(pieces) * depth
    flat = [array for piece in pieces for array in piece]
    return pl.pallas_call(
        functools.partial(line_kernel, len(pieces)),
        in_specs=[SMEM_SPEC] + [VMEM_SPEC] * len(flat),
        out_specs=[VMEM_SPEC] * count,
        out_shape=[jax.ShapeDtypeStruct((taps, lanes), F32)]
        + [jax.ShapeDtypeStruct((taps, lanes), BF16)] * (count - 1),
        scratch_shapes=[pltpu.VMEM((count, taps, lanes), F32)],
        compiler_params=params(8),
        cost_estimate=cost(4 * count * taps * lanes, 16 * count * taps * lanes),
        name="along_line",
    )(me, *flat)


def finish_kernel(factor, mine_ref, *refs):
    *got, out_ref = refs
    total = mine_ref[...]
    for ref in got:
        total = total + ref[...].astype(F32)
    out_ref[...] = (total * factor).T


def finish(mine, got, factor):
    taps, lanes = mine.shape
    return pl.pallas_call(
        functools.partial(finish_kernel, factor),
        in_specs=[VMEM_SPEC] * (1 + len(got)),
        out_specs=VMEM_SPEC,
        out_shape=jax.ShapeDtypeStruct((lanes, taps), F32),
        compiler_params=params(8),
        cost_estimate=cost(4 * taps * lanes, 16 * taps * lanes),
        name="finish",
    )(mine, *got)


def join_kernel(me_ref, mine_ref, other_ref, out_ref):
    rank = me_ref[0] % 2
    rows = mine_ref.shape[0]
    out_ref[pl.ds(pl.multiple_of(rank * rows, rows), rows), :] = mine_ref[...]
    out_ref[pl.ds(pl.multiple_of((1 - rank) * rows, rows), rows), :] = other_ref[...]


def join(me, mine, other):
    rows, taps = mine.shape
    return pl.pallas_call(
        join_kernel,
        in_specs=[SMEM_SPEC, VMEM_SPEC, VMEM_SPEC],
        out_specs=VMEM_SPEC,
        out_shape=jax.ShapeDtypeStruct((2 * rows, taps), F32),
        compiler_params=params(8),
        cost_estimate=cost(1, 16 * rows * taps),
        name="join",
    )(me, mine, other)


def tap_grad_plain_kernel(cot_ref, after_ref, val_ref, wx_ref, wv_ref, wi_ref, o_ref):
    o_ref[...] = tap_grad_tile(cot_ref, after_ref, val_ref, wx_ref, wv_ref, wi_ref)


def tap_grad_plain(cotangent, after, values, taps, tile):
    positions, channels = cotangent.shape
    wx, wv, _, wi, _ = transforms(positions, taps)
    data = pl.BlockSpec((positions, tile), lambda t: (0, t))
    whole = lambda w: pl.BlockSpec(w.shape, lambda t: (0, 0))
    return pl.pallas_call(
        tap_grad_plain_kernel,
        grid=(channels // tile,),
        in_specs=[data, data, data, whole(wx), whole(wv), whole(wi)],
        out_specs=pl.BlockSpec((taps, tile), lambda t: (0, t)),
        out_shape=jax.ShapeDtypeStruct((taps, channels), F32),
        name="tap_grad_plain",
    )(cotangent, after, values, wx, wv, wi)


def value_grad_tile(own, after, filters, wx_ref, wf_ref, wi_ref):
    x = spectrum_of_window(wx_ref[...], own, after)
    y = lax.dot_general(
        wf_ref[...],
        jnp.concatenate([filters, filters], axis=1),
        (((1,), (1,)), ((), ())),
        preferred_element_type=F32,
    )
    return correlate(x, y, wi_ref[...]).astype(BF16)


def value_grad_slots_kernel(count, me_ref, *refs):
    cots, afters = refs[:count], refs[count : 2 * count]
    mine_ref, other_ref, wx_ref, wf_ref, wi_ref, out_hbm, out_ref, sems = refs[2 * count :]
    _, depth, _, _ = mine_ref.shape
    me = me_ref[0]
    even, row, at = me // 2 % 2 == 0, me // 4 % 2, me // 8
    width = cots[0].shape[1]
    copies = []
    for piece in range(count):
        filters = []
        for z in range(piece * depth // count, (piece + 1) * depth // count):
            for y in range(2):
                mine, other = mine_ref[y ^ row, z ^ at], other_ref[y ^ row, z ^ at]
                filters += [jnp.where(even, mine, other), jnp.where(even, other, mine)]
        cols = pl.ds(piece * width, width)
        out_ref[:, cols] = value_grad_tile(
            cots[piece][...], afters[piece][...], jnp.concatenate(filters, axis=0), wx_ref, wf_ref, wi_ref
        )
        copies.append(pltpu.make_async_copy(out_ref.at[:, cols], out_hbm.at[:, cols], sems.at[piece]))
        copies[-1].start()
    for copy in copies:
        copy.wait()


def value_grad_slots(me, cotangents, afters, mine, other):
    count = len(cotangents)
    positions, width = cotangents[0].shape
    taps = mine.shape[-1]
    channels = count * width
    wx, _, wf, _, wi = transforms(positions, taps)
    return pl.pallas_call(
        functools.partial(value_grad_slots_kernel, count),
        in_specs=[SMEM_SPEC] + [VMEM_SPEC] * (2 * count + 5),
        out_specs=HBM_SPEC,
        out_shape=jax.ShapeDtypeStruct((positions, channels), BF16),
        scratch_shapes=[pltpu.VMEM((positions, channels), BF16), pltpu.SemaphoreType.DMA((count,))],
        compiler_params=params(24),
        cost_estimate=cost(2 * 9 * 128 * 256 * channels, 8 * positions * channels),
        name="value_grad_slots",
    )(me, *cotangents, *afters, mine, other, wx, wf, wi)


def value_grad_plain_kernel(cot_ref, after_ref, f_ref, wx_ref, wf_ref, wi_ref, o_ref):
    o_ref[...] = value_grad_tile(
        cot_ref[...], after_ref[...], f_ref[...], wx_ref, wf_ref, wi_ref
    )


def value_grad_plain(cotangent, after, filters, tile):
    positions, channels = cotangent.shape
    taps = filters.shape[1]
    wx, _, wf, _, wi = transforms(positions, taps)
    data = pl.BlockSpec((positions, tile), lambda t: (0, t))
    whole = lambda w: pl.BlockSpec(w.shape, lambda t: (0, 0))
    return pl.pallas_call(
        value_grad_plain_kernel,
        grid=(channels // tile,),
        in_specs=[data, data, pl.BlockSpec((tile, taps), lambda t: (t, 0)), whole(wx), whole(wf), whole(wi)],
        out_specs=data,
        out_shape=jax.ShapeDtypeStruct((positions, channels), BF16),
        name="value_grad_plain",
    )(cotangent, after, filters, wx, wf, wi)


def body(token_ids, queries, gated_values, out_grad, filters):
    queries, gated_values, out_grad = queries[0], gated_values[0], out_grad[0]
    positions, _ = queries.shape
    shard, taps = filters.shape
    seqs, parts = lax.axis_size("dp"), lax.axis_size("ctx")
    factor = float(seqs * parts * positions) ** -0.5

    staged = seqs == 2 and parts >= 8 and parts & (parts - 1) == 0 and shard == 2 * LANES
    back = [(i, i - 1) for i in range(1, parts)]
    if not staged:
        (cotangent,) = cotangent_of(token_ids, queries, out_grad, 1)
        after = lax.ppermute(cotangent, "ctx", back)
        all_filters = lax.all_gather(filters, "ctx", axis=0, tiled=True)
        value_grad = value_grad_plain(cotangent, after, all_filters, 512)
        share = tap_grad_plain(cotangent, after, gated_values, taps, 512)
        share = lax.psum_scatter(share.T * factor, "ctx", scatter_dimension=0, tiled=True)
        return value_grad[None], lax.psum(share, "dp")

    devices = seqs * parts
    depth = parts // 4
    rank = lax.axis_index("dp")
    place = lax.axis_index("ctx")
    me = (place * 2 + rank).astype(jnp.int32).reshape(1)

    def swap(x, bits):
        return lax.ppermute(x, AXES, [(i, i ^ bits) for i in range(devices)])

    def after_both(x, *others):
        return lax.optimization_barrier((x, *others))[0]

    hops = (parts, 2, parts + 2)
    cots = cotangent_of(token_ids, queries, out_grad, 2)
    afters = []
    for cot in cots:
        afters.append(lax.ppermute(cot, "ctx", back))

    filters = after_both(filters, cots[0])
    line = jnp.stack([filters] + [swap(filters, 4 * k) for k in range(1, depth)])
    afters[0] = after_both(afters[0], line)

    keep, send = tap_grad_slots(me, cots[0], afters[0], gated_values, 0, taps)
    own, *sends = spread(keep, swap(send, 1))
    sums = [[own] + [swap(x, bits) for x, bits in zip(sends, hops)]]

    afters[1], own = lax.optimization_barrier((afters[1], own))
    line_y = swap(after_both(line, afters[1]), 2)
    keep, send = tap_grad_slots(me, cots[1], afters[1], gated_values, 1, taps)
    mine = jnp.stack([line, after_both(line_y, send)])
    own, *sends = spread(keep, swap(send, 1))
    sums.append([own] + [swap(x, bits) for x, bits in zip(sends, hops)])
    other = swap(mine, 1)

    block, *sends = along_line(me, sums)
    got = [swap(x, 4 * k) for k, x in enumerate(sends, 1)]
    block = finish(block, got, factor)
    filter_grad = join(me, block, swap(block, parts))

    value_grad = value_grad_slots(me, cots, afters, mine, other)
    return value_grad[None], filter_grad


def solution(mesh):
    return jax.shard_map(
        body,
        mesh=mesh,
        in_specs=(
            P("dp", "ctx"),
            P("dp", "ctx", None),
            P("dp", "ctx", None),
            P("dp", "ctx", None),
            P("ctx", None),
        ),
        out_specs=(P("dp", "ctx", None), P("ctx", None)),
        check_vma=False,
    )
```

```python
import functools

import jax
import jax.numpy as jnp
import numpy as np
from jax import lax
from jax.experimental import pallas as pl
from jax.experimental.pallas import tpu as pltpu
from jax.sharding import PartitionSpec as P


BF16 = jnp.bfloat16
F32 = jnp.float32
AXES = ("dp", "ctx")
LANES = 128


def split_bf16(matrix):
    high = matrix.astype(BF16)
    low = (matrix - high.astype(np.float64)).astype(BF16)
    return np.asarray(high), np.asarray(low)


@functools.lru_cache(None)
def transforms(positions, taps):
    window = positions + taps
    half = window // 2
    angle = 2.0 * np.pi * np.outer(np.arange(half) + 0.5, np.arange(window)) / window
    forward = np.concatenate([np.cos(angle), np.sin(angle)], axis=0)
    high, low = split_bf16(forward)
    of_window = np.concatenate([high, low], axis=0)
    of_values = np.concatenate([high[:, :positions], low[:, :positions]], axis=1)
    of_taps = np.concatenate([high[:, :taps], low[:, :taps]], axis=1)
    inverse = forward.T / half
    inv_high, inv_low = split_bf16(inverse)
    to_taps = np.concatenate([inv_high[:taps], inv_low[:taps]], axis=0)
    to_positions = np.concatenate([inv_high[:positions], inv_low[:positions]], axis=0)
    return of_window, of_values, of_taps, to_taps, to_positions


def mul(a, b):
    return jnp.dot(a, b, preferred_element_type=F32)


def spectrum_of_window(matrix, own, after):
    both = mul(matrix, jnp.concatenate([own, after], axis=0))
    rows = both.shape[0] // 2
    return both[:rows] + both[rows:]


def correlate(x, y, inverse):
    half = x.shape[0] // 2
    a, b, c, d = x[:half], x[half:], y[:half], y[half:]
    product = jnp.concatenate([a * c + b * d, b * c - a * d], axis=0)
    high = product.astype(BF16)
    low = (product - high.astype(F32)).astype(BF16)
    rows = inverse.shape[0] // 2
    both = mul(inverse, high)
    return both[:rows] + both[rows:] + mul(inverse[:rows], low)


VMEM_SPEC = pl.BlockSpec(memory_space=pltpu.VMEM)
SMEM_SPEC = pl.BlockSpec(memory_space=pltpu.SMEM)
HBM_SPEC = pl.BlockSpec(memory_space=pltpu.HBM)


def params(mib):
    return pltpu.CompilerParams(vmem_limit_bytes=mib << 20)


def cost(flops, nbytes):
    return pl.CostEstimate(flops=flops, bytes_accessed=nbytes, transcendentals=0)


def cotangent_kernel(ids_hbm, q_hbm, g_hbm, *refs):
    *outs, ids_ref, q_ref, g_ref, sems, ids_sem = refs
    width = outs[0].shape[1]
    copies = []
    ids_copy = pltpu.make_async_copy(ids_hbm, ids_ref, ids_sem)
    ids_copy.start()
    for i in range(len(outs)):
        cols = pl.ds(i * width, width)
        copies.append(
            [
                pltpu.make_async_copy(src.at[:, cols], dst.at[:, cols], sems.at[n, i])
                for n, (src, dst) in enumerate(((q_hbm, q_ref), (g_hbm, g_ref)))
            ]
        )
        for copy in copies[-1]:
            copy.start()
    positions = ids_ref.shape[1]
    ids_copy.wait()
    weight = jnp.where(ids_ref[...] < 4, 1.0, 0.1).astype(F32)
    weight = jnp.broadcast_to(weight, (LANES, positions)).T
    for i, out in enumerate(outs):
        for copy in copies[i]:
            copy.wait()
        for at in range(0, width, LANES):
            cols = pl.ds(i * width + at, LANES)
            out[:, at : at + LANES] = (
                weight * g_ref[:, cols].astype(F32) * q_ref[:, cols].astype(F32)
            ).astype(BF16)


def cotangent_of(token_ids, queries, out_grad, pieces):
    positions, channels = queries.shape
    piece = jax.ShapeDtypeStruct((positions, channels // pieces), BF16)
    return pl.pallas_call(
        cotangent_kernel,
        in_specs=[HBM_SPEC] * 3,
        out_specs=[VMEM_SPEC] * pieces,
        out_shape=[piece] * pieces,
        scratch_shapes=[pltpu.VMEM(token_ids.shape, token_ids.dtype)]
        + [pltpu.VMEM((positions, channels), BF16)] * 2
        + [pltpu.SemaphoreType.DMA((2, pieces)), pltpu.SemaphoreType.DMA],
        compiler_params=params(8),
        cost_estimate=cost(2 * positions * channels, 6 * positions * channels),
        name="cotangent",
    )(*(pltpu.with_memory_space_constraint(x, pltpu.HBM) for x in (token_ids, queries, out_grad)))


def tap_grad_tile(cot_ref, after_ref, val_ref, wx_ref, wv_ref, wi_ref):
    x = spectrum_of_window(wx_ref[...], cot_ref[...], after_ref[...])
    values = val_ref[...]
    y = mul(wv_ref[...], jnp.concatenate([values, values], axis=0))
    return correlate(x, y, wi_ref[...])


def tap_grad_slots_kernel(
    first, me_ref, cot_ref, after_ref, val_ref, wx_ref, wv_ref, wi_ref, keep_ref, send_ref, tmp_ref
):
    width = cot_ref.shape[1]
    x = spectrum_of_window(wx_ref[...], cot_ref[...], after_ref[...])
    values = val_ref[:, first * width : (first + 1) * width]
    y = mul(wv_ref[...], jnp.concatenate([values, values], axis=0))
    out = correlate(x, y, wi_ref[...])
    low, row = me_ref[0] % 4, me_ref[0] // 4 % 2
    for tile in range(width // (4 * LANES)):
        for block in range(4):
            at = (tile * 4 + block) * LANES
            tmp_ref[tile, block ^ low] = out[:, at : at + LANES]
        for half in range(2):
            keep_ref[half, tile % 2 ^ row, tile // 2] = tmp_ref[tile, half]
            send_ref[half, tile % 2 ^ row, tile // 2] = tmp_ref[tile, 2 + half].astype(BF16)


def tap_grad_slots(me, cotangent, after, values, first, taps):
    positions, width = cotangent.shape
    wx, wv, _, wi, _ = transforms(positions, taps)
    tiles = width // (4 * LANES)
    shape = (2, 2, tiles // 2, taps, LANES)
    return pl.pallas_call(
        functools.partial(tap_grad_slots_kernel, first),
        in_specs=[SMEM_SPEC] + [VMEM_SPEC] * 6,
        out_specs=[VMEM_SPEC, VMEM_SPEC],
        out_shape=[jax.ShapeDtypeStruct(shape, F32), jax.ShapeDtypeStruct(shape, BF16)],
        scratch_shapes=[pltpu.VMEM((tiles, 4, taps, LANES), F32)],
        compiler_params=params(24),
        cost_estimate=cost(2 * 9 * 128 * 256 * width, 9 * positions * width),
        name="tap_grad_slots",
    )(me, cotangent, after, values, wx, wv, wi)


def spread_kernel(keep_ref, got_ref, mine_ref, *out_refs):
    mine_ref[...] = keep_ref[0, 0] + got_ref[0, 0].astype(F32)
    for (x, y), out_ref in zip(((1, 0), (0, 1), (1, 1)), out_refs):
        out_ref[...] = (keep_ref[x, y] + got_ref[x, y].astype(F32)).astype(BF16)


def spread(keep, got):
    block = keep.shape[2:]
    return pl.pallas_call(
        spread_kernel,
        in_specs=[VMEM_SPEC] * 2,
        out_specs=[VMEM_SPEC] * 4,
        out_shape=[jax.ShapeDtypeStruct(block, F32)] + [jax.ShapeDtypeStruct(block, BF16)] * 3,
        compiler_params=params(8),
        cost_estimate=cost(keep.size, 8 * keep.size),
        name="spread",
    )(keep, got)


def line_kernel(pieces, me_ref, *refs):
    ins, (mine_ref, *send_refs) = refs[: 4 * pieces], refs[4 * pieces : -1]
    sum_ref = refs[-1]
    depth = ins[0].shape[0]
    for piece in range(pieces):
        own, *got = ins[4 * piece : 4 * piece + 4]
        for z in range(depth):
            total = own[z]
            for ref in got:
                total = total + ref[z].astype(F32)
            sum_ref[piece * depth + z] = total
    at = me_ref[0] // 8
    mine_ref[...] = sum_ref[at]
    for k, send_ref in enumerate(send_refs, 1):
        send_ref[...] = sum_ref[at ^ k].astype(BF16)


def along_line(me, pieces):
    depth, taps, lanes = pieces[0][0].shape
    count = len(pieces) * depth
    flat = [array for piece in pieces for array in piece]
    return pl.pallas_call(
        functools.partial(line_kernel, len(pieces)),
        in_specs=[SMEM_SPEC] + [VMEM_SPEC] * len(flat),
        out_specs=[VMEM_SPEC] * count,
        out_shape=[jax.ShapeDtypeStruct((taps, lanes), F32)]
        + [jax.ShapeDtypeStruct((taps, lanes), BF16)] * (count - 1),
        scratch_shapes=[pltpu.VMEM((count, taps, lanes), F32)],
        compiler_params=params(8),
        cost_estimate=cost(4 * count * taps * lanes, 16 * count * taps * lanes),
        name="along_line",
    )(me, *flat)


def finish_kernel(factor, mine_ref, *refs):
    *got, out_ref = refs
    total = mine_ref[...]
    for ref in got:
        total = total + ref[...].astype(F32)
    out_ref[...] = (total * factor).T


def finish(mine, got, factor):
    taps, lanes = mine.shape
    return pl.pallas_call(
        functools.partial(finish_kernel, factor),
        in_specs=[VMEM_SPEC] * (1 + len(got)),
        out_specs=VMEM_SPEC,
        out_shape=jax.ShapeDtypeStruct((lanes, taps), F32),
        compiler_params=params(8),
        cost_estimate=cost(4 * taps * lanes, 16 * taps * lanes),
        name="finish",
    )(mine, *got)


def join_kernel(me_ref, mine_ref, other_ref, out_ref):
    rank = me_ref[0] % 2
    rows = mine_ref.shape[0]
    out_ref[pl.ds(pl.multiple_of(rank * rows, rows), rows), :] = mine_ref[...]
    out_ref[pl.ds(pl.multiple_of((1 - rank) * rows, rows), rows), :] = other_ref[...]


def join(me, mine, other):
    rows, taps = mine.shape
    return pl.pallas_call(
        join_kernel,
        in_specs=[SMEM_SPEC, VMEM_SPEC, VMEM_SPEC],
        out_specs=VMEM_SPEC,
        out_shape=jax.ShapeDtypeStruct((2 * rows, taps), F32),
        compiler_params=params(8),
        cost_estimate=cost(1, 16 * rows * taps),
        name="join",
    )(me, mine, other)


def tap_grad_plain_kernel(cot_ref, after_ref, val_ref, wx_ref, wv_ref, wi_ref, o_ref):
    o_ref[...] = tap_grad_tile(cot_ref, after_ref, val_ref, wx_ref, wv_ref, wi_ref)


def tap_grad_plain(cotangent, after, values, taps, tile):
    positions, channels = cotangent.shape
    wx, wv, _, wi, _ = transforms(positions, taps)
    data = pl.BlockSpec((positions, tile), lambda t: (0, t))
    whole = lambda w: pl.BlockSpec(w.shape, lambda t: (0, 0))
    return pl.pallas_call(
        tap_grad_plain_kernel,
        grid=(channels // tile,),
        in_specs=[data, data, data, whole(wx), whole(wv), whole(wi)],
        out_specs=pl.BlockSpec((taps, tile), lambda t: (0, t)),
        out_shape=jax.ShapeDtypeStruct((taps, channels), F32),
        name="tap_grad_plain",
    )(cotangent, after, values, wx, wv, wi)


def value_grad_tile(own, after, filters, wx_ref, wf_ref, wi_ref):
    x = spectrum_of_window(wx_ref[...], own, after)
    y = lax.dot_general(
        wf_ref[...],
        jnp.concatenate([filters, filters], axis=1),
        (((1,), (1,)), ((), ())),
        preferred_element_type=F32,
    )
    return correlate(x, y, wi_ref[...]).astype(BF16)


def value_grad_slots_kernel(piece, count, me_ref, *refs):
    cot_ref, after_ref, mine_ref, other_ref, wx_ref, wf_ref, wi_ref = refs[:7]
    out_hbm, out_ref, sem = refs[-3:]
    depth = mine_ref.shape[1]
    me = me_ref[0]
    even, row, at = me // 2 % 2 == 0, me // 4 % 2, me // 8
    filters = []
    for z in range(piece * depth // count, (piece + 1) * depth // count):
        for y in range(2):
            mine, other = mine_ref[y ^ row, z ^ at], other_ref[y ^ row, z ^ at]
            filters += [jnp.where(even, mine, other), jnp.where(even, other, mine)]
    out_ref[...] = value_grad_tile(
        cot_ref[...], after_ref[...], jnp.concatenate(filters, axis=0), wx_ref, wf_ref, wi_ref
    )
    width = cot_ref.shape[1]
    copy = pltpu.make_async_copy(out_ref, out_hbm.at[:, pl.ds(piece * width, width)], sem)
    copy.start()
    copy.wait()


def value_grad_slots(me, cotangent, after, mine, other, piece, count, so_far=()):
    positions, width = cotangent.shape
    taps = mine.shape[-1]
    wx, _, wf, _, wi = transforms(positions, taps)
    return pl.pallas_call(
        functools.partial(value_grad_slots_kernel, piece, count),
        in_specs=[SMEM_SPEC] + [VMEM_SPEC] * 7 + [HBM_SPEC] * len(so_far),
        out_specs=HBM_SPEC,
        out_shape=jax.ShapeDtypeStruct((positions, count * width), BF16),
        input_output_aliases={8: 0} if so_far else {},
        scratch_shapes=[pltpu.VMEM((positions, width), BF16), pltpu.SemaphoreType.DMA],
        compiler_params=params(24),
        cost_estimate=cost(2 * 9 * 128 * 256 * width, 8 * positions * width),
        name="value_grad_slots",
    )(me, cotangent, after, mine, other, wx, wf, wi, *so_far)


def value_grad_plain_kernel(cot_ref, after_ref, f_ref, wx_ref, wf_ref, wi_ref, o_ref):
    o_ref[...] = value_grad_tile(
        cot_ref[...], after_ref[...], f_ref[...], wx_ref, wf_ref, wi_ref
    )


def value_grad_plain(cotangent, after, filters, tile):
    positions, channels = cotangent.shape
    taps = filters.shape[1]
    wx, _, wf, _, wi = transforms(positions, taps)
    data = pl.BlockSpec((positions, tile), lambda t: (0, t))
    whole = lambda w: pl.BlockSpec(w.shape, lambda t: (0, 0))
    return pl.pallas_call(
        value_grad_plain_kernel,
        grid=(channels // tile,),
        in_specs=[data, data, pl.BlockSpec((tile, taps), lambda t: (t, 0)), whole(wx), whole(wf), whole(wi)],
        out_specs=data,
        out_shape=jax.ShapeDtypeStruct((positions, channels), BF16),
        name="value_grad_plain",
    )(cotangent, after, filters, wx, wf, wi)


def body(token_ids, queries, gated_values, out_grad, filters):
    queries, gated_values, out_grad = queries[0], gated_values[0], out_grad[0]
    positions, _ = queries.shape
    shard, taps = filters.shape
    seqs, parts = lax.axis_size("dp"), lax.axis_size("ctx")
    factor = float(seqs * parts * positions) ** -0.5

    staged = seqs == 2 and parts >= 8 and parts & (parts - 1) == 0 and shard == 2 * LANES
    back = [(i, i - 1) for i in range(1, parts)]
    if not staged:
        (cotangent,) = cotangent_of(token_ids, queries, out_grad, 1)
        after = lax.ppermute(cotangent, "ctx", back)
        all_filters = lax.all_gather(filters, "ctx", axis=0, tiled=True)
        value_grad = value_grad_plain(cotangent, after, all_filters, 512)
        share = tap_grad_plain(cotangent, after, gated_values, taps, 512)
        share = lax.psum_scatter(share.T * factor, "ctx", scatter_dimension=0, tiled=True)
        return value_grad[None], lax.psum(share, "dp")

    devices = seqs * parts
    depth = parts // 4
    rank = lax.axis_index("dp")
    place = lax.axis_index("ctx")
    me = (place * 2 + rank).astype(jnp.int32).reshape(1)

    def swap(x, bits):
        return lax.ppermute(x, AXES, [(i, i ^ bits) for i in range(devices)])

    def after_both(x, *others):
        return lax.optimization_barrier((x, *others))[0]

    hops = (parts, 2, parts + 2)
    cots = cotangent_of(token_ids, queries, out_grad, 2)
    afters = []
    for cot in cots:
        afters.append(lax.ppermute(cot, "ctx", back))

    filters = after_both(filters, cots[0])
    line = [filters] + [swap(filters, 4 * k) for k in range(1, depth)]

    keep, send = tap_grad_slots(me, cots[0], afters[0], gated_values, 0, taps)
    own, *sends = spread(keep, swap(send, 1))
    sums = [[own] + [swap(x, bits) for x, bits in zip(sends, hops)]]

    afters[1], own = lax.optimization_barrier((afters[1], own))
    line = jnp.stack(lax.optimization_barrier((*line, own))[:-1])
    line_y = swap(after_both(line, afters[1]), 2)
    keep, send = tap_grad_slots(me, cots[1], afters[1], gated_values, 1, taps)
    mine = jnp.stack([line, after_both(line_y, send)])
    own, *sends = spread(keep, swap(send, 1))
    sums.append([own] + [swap(x, bits) for x, bits in zip(sends, hops)])
    other = swap(mine, 1)

    block, *sends = along_line(me, sums)
    got = [swap(x, 4 * k) for k, x in enumerate(sends, 1)]
    block = finish(block, got, factor)
    filter_grad = join(me, block, swap(block, parts))

    value_grad = ()
    for piece in range(2):
        value_grad = [
            value_grad_slots(me, cots[piece], afters[piece], mine, other, piece, 2, value_grad)
        ]
    value_grad = value_grad[0]
    return value_grad[None], filter_grad


def solution(mesh):
    return jax.shard_map(
        body,
        mesh=mesh,
        in_specs=(
            P("dp", "ctx"),
            P("dp", "ctx", None),
            P("dp", "ctx", None),
            P("dp", "ctx", None),
            P("ctx", None),
        ),
        out_specs=(P("dp", "ctx", None), P("ctx", None)),
        check_vma=False,
    )
```

```python
import functools

import jax
import jax.numpy as jnp
import numpy as np
from jax import lax
from jax.experimental import pallas as pl
from jax.experimental.pallas import tpu as pltpu
from jax.sharding import PartitionSpec as P


BF16 = jnp.bfloat16
F32 = jnp.float32
AXES = ("dp", "ctx")
LANES = 128


def split_bf16(matrix):
    high = matrix.astype(BF16)
    low = (matrix - high.astype(np.float64)).astype(BF16)
    return np.asarray(high), np.asarray(low)


@functools.lru_cache(None)
def transforms(positions, taps):
    window = positions + taps
    half = window // 2
    angle = 2.0 * np.pi * np.outer(np.arange(half) + 0.5, np.arange(window)) / window
    forward = np.concatenate([np.cos(angle), np.sin(angle)], axis=0)
    high, low = split_bf16(forward)
    of_window = np.concatenate([high, low], axis=0)
    of_values = np.concatenate([high[:, :positions], low[:, :positions]], axis=1)
    of_taps = np.concatenate([high[:, :taps], low[:, :taps]], axis=1)
    inverse = forward.T / half
    inv_high, inv_low = split_bf16(inverse)
    to_taps = np.concatenate([inv_high[:taps], inv_low[:taps]], axis=0)
    to_positions = np.concatenate([inv_high[:positions], inv_low[:positions]], axis=0)
    return of_window, of_values, of_taps, to_taps, to_positions


def mul(a, b):
    return jnp.dot(a, b, preferred_element_type=F32)


def spectrum_of_window(matrix, own, after):
    both = mul(matrix, jnp.concatenate([own, after], axis=0))
    rows = both.shape[0] // 2
    return both[:rows] + both[rows:]


def correlate(x, y, inverse):
    half = x.shape[0] // 2
    a, b, c, d = x[:half], x[half:], y[:half], y[half:]
    product = jnp.concatenate([a * c + b * d, b * c - a * d], axis=0)
    high = product.astype(BF16)
    low = (product - high.astype(F32)).astype(BF16)
    rows = inverse.shape[0] // 2
    both = mul(inverse, high)
    return both[:rows] + both[rows:] + mul(inverse[:rows], low)


VMEM_SPEC = pl.BlockSpec(memory_space=pltpu.VMEM)
SMEM_SPEC = pl.BlockSpec(memory_space=pltpu.SMEM)
HBM_SPEC = pl.BlockSpec(memory_space=pltpu.HBM)


def params(mib):
    return pltpu.CompilerParams(vmem_limit_bytes=mib << 20)


def cost(flops, nbytes):
    return pl.CostEstimate(flops=flops, bytes_accessed=nbytes, transcendentals=0)


def cotangent_kernel(ids_hbm, q_hbm, g_hbm, *refs):
    *outs, ids_ref, q_ref, g_ref, sems, ids_sem = refs
    width = outs[0].shape[1]
    copies = []
    ids_copy = pltpu.make_async_copy(ids_hbm, ids_ref, ids_sem)
    ids_copy.start()
    for i in range(len(outs)):
        cols = pl.ds(i * width, width)
        copies.append(
            [
                pltpu.make_async_copy(src.at[:, cols], dst.at[:, cols], sems.at[n, i])
                for n, (src, dst) in enumerate(((q_hbm, q_ref), (g_hbm, g_ref)))
            ]
        )
        for copy in copies[-1]:
            copy.start()
    positions = ids_ref.shape[1]
    ids_copy.wait()
    weight = jnp.where(ids_ref[...] < 4, 1.0, 0.1).astype(F32)
    weight = jnp.broadcast_to(weight, (LANES, positions)).T
    for i, out in enumerate(outs):
        for copy in copies[i]:
            copy.wait()
        for at in range(0, width, LANES):
            cols = pl.ds(i * width + at, LANES)
            out[:, at : at + LANES] = (
                weight * g_ref[:, cols].astype(F32) * q_ref[:, cols].astype(F32)
            ).astype(BF16)


def cotangent_of(token_ids, queries, out_grad, pieces):
    positions, channels = queries.shape
    piece = jax.ShapeDtypeStruct((positions, channels // pieces), BF16)
    return pl.pallas_call(
        cotangent_kernel,
        in_specs=[HBM_SPEC] * 3,
        out_specs=[VMEM_SPEC] * pieces,
        out_shape=[piece] * pieces,
        scratch_shapes=[pltpu.VMEM(token_ids.shape, token_ids.dtype)]
        + [pltpu.VMEM((positions, channels), BF16)] * 2
        + [pltpu.SemaphoreType.DMA((2, pieces)), pltpu.SemaphoreType.DMA],
        compiler_params=params(8),
        cost_estimate=cost(2 * positions * channels, 6 * positions * channels),
        name="cotangent",
    )(*(pltpu.with_memory_space_constraint(x, pltpu.HBM) for x in (token_ids, queries, out_grad)))


def tap_grad_tile(cot_ref, after_ref, val_ref, wx_ref, wv_ref, wi_ref):
    x = spectrum_of_window(wx_ref[...], cot_ref[...], after_ref[...])
    values = val_ref[...]
    y = mul(wv_ref[...], jnp.concatenate([values, values], axis=0))
    return correlate(x, y, wi_ref[...])


def tap_grad_slots_kernel(
    first, me_ref, cot_ref, after_ref, val_ref, wx_ref, wv_ref, wi_ref, keep_ref, send_ref, tmp_ref
):
    width = cot_ref.shape[1]
    x = spectrum_of_window(wx_ref[...], cot_ref[...], after_ref[...])
    values = val_ref[:, first * width : (first + 1) * width]
    y = mul(wv_ref[...], jnp.concatenate([values, values], axis=0))
    out = correlate(x, y, wi_ref[...])
    low, row = me_ref[0] % 4, me_ref[0] // 4 % 2
    for tile in range(width // (4 * LANES)):
        for block in range(4):
            at = (tile * 4 + block) * LANES
            tmp_ref[tile, block ^ low] = out[:, at : at + LANES]
        for half in range(2):
            keep_ref[half, tile % 2 ^ row, tile // 2] = tmp_ref[tile, half]
            send_ref[half, tile % 2 ^ row, tile // 2] = tmp_ref[tile, 2 + half].astype(BF16)


def tap_grad_slots(me, cotangent, after, values, first, taps):
    positions, width = cotangent.shape
    wx, wv, _, wi, _ = transforms(positions, taps)
    tiles = width // (4 * LANES)
    shape = (2, 2, tiles // 2, taps, LANES)
    return pl.pallas_call(
        functools.partial(tap_grad_slots_kernel, first),
        in_specs=[SMEM_SPEC] + [VMEM_SPEC] * 6,
        out_specs=[VMEM_SPEC, VMEM_SPEC],
        out_shape=[jax.ShapeDtypeStruct(shape, F32), jax.ShapeDtypeStruct(shape, BF16)],
        scratch_shapes=[pltpu.VMEM((tiles, 4, taps, LANES), F32)],
        compiler_params=params(24),
        cost_estimate=cost(2 * 9 * 128 * 256 * width, 9 * positions * width),
        name="tap_grad_slots",
    )(me, cotangent, after, values, wx, wv, wi)


def collect_kernel(*refs):
    *ins, out_ref = refs
    for i, ref in enumerate(ins):
        out_ref[i] = ref[...]


def collect(arrays):
    first = arrays[0]
    return pl.pallas_call(
        collect_kernel,
        in_specs=[VMEM_SPEC] * len(arrays),
        out_specs=VMEM_SPEC,
        out_shape=jax.ShapeDtypeStruct((len(arrays), *first.shape), first.dtype),
        compiler_params=params(8),
        cost_estimate=cost(1, 4 * len(arrays) * first.size),
        name="collect",
    )(*arrays)


def spread_kernel(keep_ref, got_ref, mine_ref, *out_refs):
    mine_ref[...] = keep_ref[0, 0] + got_ref[0, 0].astype(F32)
    for (x, y), out_ref in zip(((1, 0), (0, 1), (1, 1)), out_refs):
        out_ref[...] = (keep_ref[x, y] + got_ref[x, y].astype(F32)).astype(BF16)


def spread(keep, got):
    block = keep.shape[2:]
    return pl.pallas_call(
        spread_kernel,
        in_specs=[VMEM_SPEC] * 2,
        out_specs=[VMEM_SPEC] * 4,
        out_shape=[jax.ShapeDtypeStruct(block, F32)] + [jax.ShapeDtypeStruct(block, BF16)] * 3,
        compiler_params=params(8),
        cost_estimate=cost(keep.size, 8 * keep.size),
        name="spread",
    )(keep, got)


def line_kernel(pieces, me_ref, *refs):
    ins, (mine_ref, *send_refs) = refs[: 4 * pieces], refs[4 * pieces : -1]
    sum_ref = refs[-1]
    depth = ins[0].shape[0]
    for piece in range(pieces):
        own, *got = ins[4 * piece : 4 * piece + 4]
        for z in range(depth):
            total = own[z]
            for ref in got:
                total = total + ref[z].astype(F32)
            sum_ref[piece * depth + z] = total
    at = me_ref[0] // 8
    mine_ref[...] = sum_ref[at]
    for k, send_ref in enumerate(send_refs, 1):
        send_ref[...] = sum_ref[at ^ k].astype(BF16)


def along_line(me, pieces):
    depth, taps, lanes = pieces[0][0].shape
    count = len(pieces) * depth
    flat = [array for piece in pieces for array in piece]
    return pl.pallas_call(
        functools.partial(line_kernel, len(pieces)),
        in_specs=[SMEM_SPEC] + [VMEM_SPEC] * len(flat),
        out_specs=[VMEM_SPEC] * count,
        out_shape=[jax.ShapeDtypeStruct((taps, lanes), F32)]
        + [jax.ShapeDtypeStruct((taps, lanes), BF16)] * (count - 1),
        scratch_shapes=[pltpu.VMEM((count, taps, lanes), F32)],
        compiler_params=params(8),
        cost_estimate=cost(4 * count * taps * lanes, 16 * count * taps * lanes),
        name="along_line",
    )(me, *flat)


def finish_kernel(factor, mine_ref, *refs):
    *got, out_ref = refs
    total = mine_ref[...]
    for ref in got:
        total = total + ref[...].astype(F32)
    out_ref[...] = (total * factor).T


def finish(mine, got, factor):
    taps, lanes = mine.shape
    return pl.pallas_call(
        functools.partial(finish_kernel, factor),
        in_specs=[VMEM_SPEC] * (1 + len(got)),
        out_specs=VMEM_SPEC,
        out_shape=jax.ShapeDtypeStruct((lanes, taps), F32),
        compiler_params=params(8),
        cost_estimate=cost(4 * taps * lanes, 16 * taps * lanes),
        name="finish",
    )(mine, *got)


def join_kernel(me_ref, mine_ref, other_ref, out_ref):
    rank = me_ref[0] % 2
    rows = mine_ref.shape[0]
    out_ref[pl.ds(pl.multiple_of(rank * rows, rows), rows), :] = mine_ref[...]
    out_ref[pl.ds(pl.multiple_of((1 - rank) * rows, rows), rows), :] = other_ref[...]


def join(me, mine, other):
    rows, taps = mine.shape
    return pl.pallas_call(
        join_kernel,
        in_specs=[SMEM_SPEC, VMEM_SPEC, VMEM_SPEC],
        out_specs=VMEM_SPEC,
        out_shape=jax.ShapeDtypeStruct((2 * rows, taps), F32),
        compiler_params=params(8),
        cost_estimate=cost(1, 16 * rows * taps),
        name="join",
    )(me, mine, other)


def tap_grad_plain_kernel(cot_ref, after_ref, val_ref, wx_ref, wv_ref, wi_ref, o_ref):
    o_ref[...] = tap_grad_tile(cot_ref, after_ref, val_ref, wx_ref, wv_ref, wi_ref)


def tap_grad_plain(cotangent, after, values, taps, tile):
    positions, channels = cotangent.shape
    wx, wv, _, wi, _ = transforms(positions, taps)
    data = pl.BlockSpec((positions, tile), lambda t: (0, t))
    whole = lambda w: pl.BlockSpec(w.shape, lambda t: (0, 0))
    return pl.pallas_call(
        tap_grad_plain_kernel,
        grid=(channels // tile,),
        in_specs=[data, data, data, whole(wx), whole(wv), whole(wi)],
        out_specs=pl.BlockSpec((taps, tile), lambda t: (0, t)),
        out_shape=jax.ShapeDtypeStruct((taps, channels), F32),
        name="tap_grad_plain",
    )(cotangent, after, values, wx, wv, wi)


def value_grad_tile(own, after, filters, wx_ref, wf_ref, wi_ref):
    x = spectrum_of_window(wx_ref[...], own, after)
    y = lax.dot_general(
        wf_ref[...],
        jnp.concatenate([filters, filters], axis=1),
        (((1,), (1,)), ((), ())),
        preferred_element_type=F32,
    )
    return correlate(x, y, wi_ref[...]).astype(BF16)


def value_grad_slots_kernel(piece, count, me_ref, *refs):
    cot_ref, after_ref, mine_ref, other_ref, wx_ref, wf_ref, wi_ref = refs[:7]
    out_hbm, out_ref, sem = refs[-3:]
    depth = mine_ref.shape[1]
    me = me_ref[0]
    even, row, at = me // 2 % 2 == 0, me // 4 % 2, me // 8
    filters = []
    for z in range(piece * depth // count, (piece + 1) * depth // count):
        for y in range(2):
            mine, other = mine_ref[y ^ row, z ^ at], other_ref[y ^ row, z ^ at]
            filters += [jnp.where(even, mine, other), jnp.where(even, other, mine)]
    out_ref[...] = value_grad_tile(
        cot_ref[...], after_ref[...], jnp.concatenate(filters, axis=0), wx_ref, wf_ref, wi_ref
    )
    width = cot_ref.shape[1]
    copy = pltpu.make_async_copy(out_ref, out_hbm.at[:, pl.ds(piece * width, width)], sem)
    copy.start()
    copy.wait()


def value_grad_slots(me, cotangent, after, mine, other, piece, count, so_far=()):
    positions, width = cotangent.shape
    taps = mine.shape[-1]
    wx, _, wf, _, wi = transforms(positions, taps)
    return pl.pallas_call(
        functools.partial(value_grad_slots_kernel, piece, count),
        in_specs=[SMEM_SPEC] + [VMEM_SPEC] * 7 + [HBM_SPEC] * len(so_far),
        out_specs=HBM_SPEC,
        out_shape=jax.ShapeDtypeStruct((positions, count * width), BF16),
        input_output_aliases={8: 0} if so_far else {},
        scratch_shapes=[pltpu.VMEM((positions, width), BF16), pltpu.SemaphoreType.DMA],
        compiler_params=params(24),
        cost_estimate=cost(2 * 9 * 128 * 256 * width, 8 * positions * width),
        name="value_grad_slots",
    )(me, cotangent, after, mine, other, wx, wf, wi, *so_far)


def value_grad_plain_kernel(cot_ref, after_ref, f_ref, wx_ref, wf_ref, wi_ref, o_ref):
    o_ref[...] = value_grad_tile(
        cot_ref[...], after_ref[...], f_ref[...], wx_ref, wf_ref, wi_ref
    )


def value_grad_plain(cotangent, after, filters, tile):
    positions, channels = cotangent.shape
    taps = filters.shape[1]
    wx, _, wf, _, wi = transforms(positions, taps)
    data = pl.BlockSpec((positions, tile), lambda t: (0, t))
    whole = lambda w: pl.BlockSpec(w.shape, lambda t: (0, 0))
    return pl.pallas_call(
        value_grad_plain_kernel,
        grid=(channels // tile,),
        in_specs=[data, data, pl.BlockSpec((tile, taps), lambda t: (t, 0)), whole(wx), whole(wf), whole(wi)],
        out_specs=data,
        out_shape=jax.ShapeDtypeStruct((positions, channels), BF16),
        name="value_grad_plain",
    )(cotangent, after, filters, wx, wf, wi)


def body(token_ids, queries, gated_values, out_grad, filters):
    queries, gated_values, out_grad = queries[0], gated_values[0], out_grad[0]
    positions, _ = queries.shape
    shard, taps = filters.shape
    seqs, parts = lax.axis_size("dp"), lax.axis_size("ctx")
    factor = float(seqs * parts * positions) ** -0.5

    staged = seqs == 2 and parts >= 8 and parts & (parts - 1) == 0 and shard == 2 * LANES
    back = [(i, i - 1) for i in range(1, parts)]
    if not staged:
        (cotangent,) = cotangent_of(token_ids, queries, out_grad, 1)
        after = lax.ppermute(cotangent, "ctx", back)
        all_filters = lax.all_gather(filters, "ctx", axis=0, tiled=True)
        value_grad = value_grad_plain(cotangent, after, all_filters, 512)
        share = tap_grad_plain(cotangent, after, gated_values, taps, 512)
        share = lax.psum_scatter(share.T * factor, "ctx", scatter_dimension=0, tiled=True)
        return value_grad[None], lax.psum(share, "dp")

    devices = seqs * parts
    depth = parts // 4
    rank = lax.axis_index("dp")
    place = lax.axis_index("ctx")
    me = (place * 2 + rank).astype(jnp.int32).reshape(1)

    def swap(x, bits):
        return lax.ppermute(x, AXES, [(i, i ^ bits) for i in range(devices)])

    hops = (parts, 2, parts + 2)
    line = [filters] + [swap(filters, 4 * k) for k in range(1, depth)]

    cots = cotangent_of(token_ids, queries, out_grad, 2)
    afters = []
    for cot in cots:
        afters.append(lax.ppermute(cot, "ctx", back))

    keep, send = tap_grad_slots(me, cots[0], afters[0], gated_values, 0, taps)
    own, *sends = spread(keep, swap(send, 1))
    sums = [[own] + [swap(x, bits) for x, bits in zip(sends, hops)]]

    line = collect(line)
    line_y = swap(line, 2)
    keep, send = tap_grad_slots(me, cots[1], afters[1], gated_values, 1, taps)
    mine = collect([line, line_y])
    own, *sends = spread(keep, swap(send, 1))
    sums.append([own] + [swap(x, bits) for x, bits in zip(sends, hops)])
    other = swap(mine, 1)

    block, *sends = along_line(me, sums)
    got = [swap(x, 4 * k) for k, x in enumerate(sends, 1)]
    block = finish(block, got, factor)
    filter_grad = join(me, block, swap(block, parts))

    value_grad = ()
    for piece in range(2):
        value_grad = [
            value_grad_slots(me, cots[piece], afters[piece], mine, other, piece, 2, value_grad)
        ]
    value_grad = value_grad[0]
    return value_grad[None], filter_grad


def solution(mesh):
    return jax.shard_map(
        body,
        mesh=mesh,
        in_specs=(
            P("dp", "ctx"),
            P("dp", "ctx", None),
            P("dp", "ctx", None),
            P("dp", "ctx", None),
            P("ctx", None),
        ),
        out_specs=(P("dp", "ctx", None), P("ctx", None)),
        check_vma=False,
    )
```

```python
import functools

import jax
import jax.numpy as jnp
import numpy as np
from jax import lax
from jax.experimental import pallas as pl
from jax.experimental.pallas import tpu as pltpu
from jax.sharding import PartitionSpec as P


BF16 = jnp.bfloat16
F32 = jnp.float32
AXES = ("dp", "ctx")
LANES = 128


def split_bf16(matrix):
    high = matrix.astype(BF16)
    low = (matrix - high.astype(np.float64)).astype(BF16)
    return np.asarray(high), np.asarray(low)


@functools.lru_cache(None)
def transforms(positions, taps):
    window = positions + taps
    half = window // 2
    angle = 2.0 * np.pi * np.outer(np.arange(half) + 0.5, np.arange(window)) / window
    forward = np.concatenate([np.cos(angle), np.sin(angle)], axis=0)
    high, low = split_bf16(forward)
    of_window = np.concatenate([high, low], axis=0)
    of_values = np.concatenate([high[:, :positions], low[:, :positions]], axis=1)
    of_taps = np.concatenate([high[:, :taps], low[:, :taps]], axis=1)
    inverse = forward.T / half
    inv_high, inv_low = split_bf16(inverse)
    to_taps = np.concatenate([inv_high[:taps], inv_low[:taps]], axis=0)
    to_positions = np.concatenate([inv_high[:positions], inv_low[:positions]], axis=0)
    return of_window, of_values, of_taps, to_taps, to_positions


def mul(a, b):
    return jnp.dot(a, b, preferred_element_type=F32)


def spectrum_of_window(matrix, own, after):
    both = mul(matrix, jnp.concatenate([own, after], axis=0))
    rows = both.shape[0] // 2
    return both[:rows] + both[rows:]


def cross(x, y):
    half = x.shape[0] // 2
    a, b, c, d = x[:half], x[half:], y[:half], y[half:]
    return jnp.concatenate([a * c + b * d, b * c - a * d], axis=0)


def inverted(product, inverse):
    high = product.astype(BF16)
    low = (product - high.astype(F32)).astype(BF16)
    rows = inverse.shape[0] // 2
    both = mul(inverse, high)
    return both[:rows] + both[rows:] + mul(inverse[:rows], low)


def spectrum_of_values(matrix, values):
    return mul(matrix, jnp.concatenate([values, values], axis=0))


VMEM_SPEC = pl.BlockSpec(memory_space=pltpu.VMEM)
SMEM_SPEC = pl.BlockSpec(memory_space=pltpu.SMEM)
HBM_SPEC = pl.BlockSpec(memory_space=pltpu.HBM)


def params(mib):
    return pltpu.CompilerParams(vmem_limit_bytes=mib << 20)


def cost(flops, nbytes):
    return pl.CostEstimate(flops=flops, bytes_accessed=nbytes, transcendentals=0)


def cotangent_kernel(ids_hbm, q_hbm, g_hbm, *refs):
    *outs, ids_ref, q_ref, g_ref, sems, ids_sem = refs
    width = outs[0].shape[1]
    copies = []
    ids_copy = pltpu.make_async_copy(ids_hbm, ids_ref, ids_sem)
    ids_copy.start()
    for i in range(len(outs)):
        cols = pl.ds(i * width, width)
        copies.append(
            [
                pltpu.make_async_copy(src.at[:, cols], dst.at[:, cols], sems.at[n, i])
                for n, (src, dst) in enumerate(((q_hbm, q_ref), (g_hbm, g_ref)))
            ]
        )
        for copy in copies[-1]:
            copy.start()
    positions = ids_ref.shape[1]
    ids_copy.wait()
    weight = jnp.where(ids_ref[...] < 4, 1.0, 0.1).astype(F32)
    weight = jnp.broadcast_to(weight, (LANES, positions)).T
    for i, out in enumerate(outs):
        for copy in copies[i]:
            copy.wait()
        for at in range(0, width, LANES):
            cols = pl.ds(i * width + at, LANES)
            out[:, at : at + LANES] = (
                weight * g_ref[:, cols].astype(F32) * q_ref[:, cols].astype(F32)
            ).astype(BF16)


def cotangent_of(token_ids, queries, out_grad, pieces):
    positions, channels = queries.shape
    piece = jax.ShapeDtypeStruct((positions, channels // pieces), BF16)
    return pl.pallas_call(
        cotangent_kernel,
        in_specs=[HBM_SPEC] * 3,
        out_specs=[VMEM_SPEC] * pieces,
        out_shape=[piece] * pieces,
        scratch_shapes=[pltpu.VMEM(token_ids.shape, token_ids.dtype)]
        + [pltpu.VMEM((positions, channels), BF16)] * 2
        + [pltpu.SemaphoreType.DMA((2, pieces)), pltpu.SemaphoreType.DMA],
        compiler_params=params(8),
        cost_estimate=cost(2 * positions * channels, 6 * positions * channels),
        name="cotangent",
    )(*(pltpu.with_memory_space_constraint(x, pltpu.HBM) for x in (token_ids, queries, out_grad)))


def cotangent_pair_kernel(pieces, shard, me_ref, ids_hbm, q_hbm, g_hbm, *refs):
    halos, (own_ref, other_ref) = refs[: 2 * pieces], refs[2 * pieces : 2 * pieces + 2]
    ids_ref, q_ref, g_ref, sems, ids_sem = refs[2 * pieces + 2 :]
    core0 = me_ref[0] // 2 % 2 == 0
    width = q_ref.shape[1] // pieces
    copies = []
    ids_copy = pltpu.make_async_copy(ids_hbm, ids_ref, ids_sem)
    ids_copy.start()
    for i in range(pieces):
        cols = pl.ds(i * width, width)
        copies.append(
            [
                pltpu.make_async_copy(src.at[:, cols], dst.at[:, cols], sems.at[n, i])
                for n, (src, dst) in enumerate(((q_hbm, q_ref), (g_hbm, g_ref)))
            ]
        )
        for copy in copies[-1]:
            copy.start()
    positions = ids_ref.shape[1]
    ids_copy.wait()
    weight = jnp.where(ids_ref[...] < 4, 1.0, 0.1).astype(F32)
    weight = jnp.broadcast_to(weight, (LANES, positions)).T

    def cotangent(at):
        cols = pl.ds(at, LANES)
        return (weight * g_ref[:, cols].astype(F32) * q_ref[:, cols].astype(F32)).astype(BF16)

    for i in range(pieces):
        for copy in copies[i]:
            copy.wait()
        for at in range(0, width // 2, LANES):
            source = i * width + at // shard * 2 * shard + at % shard
            even, odd = cotangent(source), cotangent(source + shard)
            halos[2 * i][:, at : at + LANES] = even
            halos[2 * i + 1][:, at : at + LANES] = odd
            cols = pl.ds(i * width // 2 + at, LANES)
            own_ref[:, cols] = jnp.where(core0, even, odd)
            other_ref[:, cols] = jnp.where(core0, odd, even)


def cotangent_pair(me, token_ids, queries, out_grad, pieces, shard):
    positions, channels = queries.shape
    piece = jax.ShapeDtypeStruct((positions, channels // 2 // pieces), BF16)
    half = jax.ShapeDtypeStruct((positions, channels // 2), BF16)
    return pl.pallas_call(
        functools.partial(cotangent_pair_kernel, pieces, shard),
        in_specs=[SMEM_SPEC] + [HBM_SPEC] * 3,
        out_specs=[VMEM_SPEC] * (2 * pieces + 2),
        out_shape=[piece] * (2 * pieces) + [half] * 2,
        scratch_shapes=[pltpu.VMEM(token_ids.shape, token_ids.dtype)]
        + [pltpu.VMEM((positions, channels), BF16)] * 2
        + [pltpu.SemaphoreType.DMA((2, pieces)), pltpu.SemaphoreType.DMA],
        compiler_params=params(8),
        cost_estimate=cost(2 * positions * channels, 8 * positions * channels),
        name="cotangent_pair",
    )(me, *(pltpu.with_memory_space_constraint(x, pltpu.HBM) for x in (token_ids, queries, out_grad)))


def split_kernel(shard, me_ref, src_hbm, own_ref, other_ref, sems):
    core = me_ref[0] // 2 % 2
    copies = []
    for n, (parity, ref) in enumerate(((core, own_ref), (1 - core, other_ref))):
        for at in range(0, own_ref.shape[1], shard):
            cols = pl.ds(pl.multiple_of(2 * at + parity * shard, shard), shard)
            copy = pltpu.make_async_copy(
                src_hbm.at[:, cols], ref.at[:, pl.ds(at, shard)], sems.at[n, at // shard]
            )
            copy.start()
            copies.append(copy)
    for copy in copies:
        copy.wait()


def split(me, values, shard):
    positions, channels = values.shape
    half = jax.ShapeDtypeStruct((positions, channels // 2), values.dtype)
    return pl.pallas_call(
        functools.partial(split_kernel, shard),
        in_specs=[SMEM_SPEC, HBM_SPEC],
        out_specs=[VMEM_SPEC] * 2,
        out_shape=[half] * 2,
        scratch_shapes=[pltpu.SemaphoreType.DMA((2, channels // 2 // shard))],
        compiler_params=params(8),
        cost_estimate=cost(1, 4 * positions * channels),
        name="split",
    )(me, pltpu.with_memory_space_constraint(values, pltpu.HBM))


def near_window_kernel(
    me_ref, own_ref, got_ref, val_ref, val_got_ref, wx_ref, wv_ref, x_ref, product_ref, v_ref
):
    core0 = me_ref[0] // 2 % 2 == 0
    own, got = own_ref[...], got_ref[...]
    x = spectrum_of_window(wx_ref[...], jnp.where(core0, own, got), jnp.where(core0, got, own))
    x_ref[...] = x
    own, got = val_ref[...], val_got_ref[...]
    v_ref[...] = spectrum_of_values(wv_ref[...], jnp.where(core0, got, own))
    product_ref[...] = cross(x, spectrum_of_values(wv_ref[...], jnp.where(core0, own, got)))


def near_window(me, own, got, values, values_got, taps):
    positions, width = own.shape
    wx, wv, _, _, _ = transforms(positions, taps)
    spectrum = jax.ShapeDtypeStruct((wx.shape[1], width), F32)
    return pl.pallas_call(
        near_window_kernel,
        in_specs=[SMEM_SPEC] + [VMEM_SPEC] * 6,
        out_specs=[VMEM_SPEC] * 3,
        out_shape=[spectrum] * 3,
        compiler_params=params(24),
        cost_estimate=cost(2 * 8 * 128 * 256 * width, 32 * positions * width),
        name="near_window",
    )(me, own, got, values, values_got, wx, wv)


def tap_grad_kernel(
    piece, me_ref, own_ref, got_ref, after0_ref, after1_ref, product_ref, v_ref, wx_ref, wi_ref, *refs
):
    mine_ref, *send_refs, x_ref, tmp_ref = refs
    width = after0_ref.shape[1]
    cols = pl.ds(piece * width, width)
    me = me_ref[0]
    core0, row, rank = me // 2 % 2 == 0, me // 4 % 2, me % 2
    own = jnp.where(core0, got_ref[:, cols], own_ref[:, cols])
    after = jnp.where(core0, after0_ref[...], after1_ref[...])
    x = spectrum_of_window(wx_ref[...], own, after)
    x_ref[...] = x
    out = inverted(product_ref[:, cols] + cross(x, v_ref[:, cols]), wi_ref[...])
    for block in range(width // LANES):
        half, y, z = block % 2, block // 2 % 2, block // 4
        tmp_ref[(half ^ rank) + 2 * (y ^ row), z] = out[:, block * LANES : (block + 1) * LANES]
    mine_ref[...] = tmp_ref[0]
    for k, ref in enumerate(send_refs, 1):
        ref[...] = tmp_ref[k].astype(BF16)


def tap_grad(me, own, got, afters, product, v, piece, taps):
    positions, width = afters[0].shape
    wx, _, _, wi, _ = transforms(positions, taps)
    depth = width // (4 * LANES)
    block = (depth, taps, LANES)
    return pl.pallas_call(
        functools.partial(tap_grad_kernel, piece),
        in_specs=[SMEM_SPEC] + [VMEM_SPEC] * 8,
        out_specs=[VMEM_SPEC] * 5,
        out_shape=[jax.ShapeDtypeStruct(block, F32)]
        + [jax.ShapeDtypeStruct(block, BF16)] * 3
        + [jax.ShapeDtypeStruct((wx.shape[1], width), F32)],
        scratch_shapes=[pltpu.VMEM((4, *block), F32)],
        compiler_params=params(24),
        cost_estimate=cost(2 * 7 * 128 * 256 * width, 24 * positions * width),
        name="tap_grad",
    )(me, own, got, *afters, product, v, wx, wi)


def collect_kernel(*refs):
    *ins, out_ref = refs
    for i, ref in enumerate(ins):
        out_ref[i] = ref[...]


def collect(arrays):
    first = arrays[0]
    return pl.pallas_call(
        collect_kernel,
        in_specs=[VMEM_SPEC] * len(arrays),
        out_specs=VMEM_SPEC,
        out_shape=jax.ShapeDtypeStruct((len(arrays), *first.shape), first.dtype),
        compiler_params=params(8),
        cost_estimate=cost(1, 4 * len(arrays) * first.size),
        name="collect",
    )(*arrays)


def line_kernel(pieces, me_ref, *refs):
    ins, (mine_ref, *send_refs) = refs[: 4 * pieces], refs[4 * pieces : -1]
    sum_ref = refs[-1]
    depth = ins[0].shape[0]
    for piece in range(pieces):
        own, *got = ins[4 * piece : 4 * piece + 4]
        for z in range(depth):
            total = own[z]
            for ref in got:
                total = total + ref[z].astype(F32)
            sum_ref[piece * depth + z] = total
    at = me_ref[0] // 8
    mine_ref[...] = sum_ref[at]
    for k, send_ref in enumerate(send_refs, 1):
        send_ref[...] = sum_ref[at ^ k].astype(BF16)


def along_line(me, pieces):
    depth, taps, lanes = pieces[0][0].shape
    count = len(pieces) * depth
    flat = [array for piece in pieces for array in piece]
    return pl.pallas_call(
        functools.partial(line_kernel, len(pieces)),
        in_specs=[SMEM_SPEC] + [VMEM_SPEC] * len(flat),
        out_specs=[VMEM_SPEC] * count,
        out_shape=[jax.ShapeDtypeStruct((taps, lanes), F32)]
        + [jax.ShapeDtypeStruct((taps, lanes), BF16)] * (count - 1),
        scratch_shapes=[pltpu.VMEM((count, taps, lanes), F32)],
        compiler_params=params(8),
        cost_estimate=cost(4 * count * taps * lanes, 16 * count * taps * lanes),
        name="along_line",
    )(me, *flat)


def finish_kernel(factor, mine_ref, *refs):
    *got, out_ref = refs
    total = mine_ref[...]
    for ref in got:
        total = total + ref[...].astype(F32)
    out_ref[...] = (total * factor).T


def finish(mine, got, factor):
    taps, lanes = mine.shape
    return pl.pallas_call(
        functools.partial(finish_kernel, factor),
        in_specs=[VMEM_SPEC] * (1 + len(got)),
        out_specs=VMEM_SPEC,
        out_shape=jax.ShapeDtypeStruct((lanes, taps), F32),
        compiler_params=params(8),
        cost_estimate=cost(4 * taps * lanes, 16 * taps * lanes),
        name="finish",
    )(mine, *got)


def place_kernel(shard, me_ref, tap_ref, tap_got_ref, val_ref, val_got_ref, val_hbm, tap_hbm, sems, tap_sems):
    core, rank = me_ref[0] // 2 % 2, me_ref[0] % 2
    rows = tap_ref.shape[0]
    copies = []
    for n, (half, ref) in enumerate(((rank, tap_ref), (1 - rank, tap_got_ref))):
        at = pl.ds(pl.multiple_of(half * rows, rows), rows)
        copies.append(pltpu.make_async_copy(ref, tap_hbm.at[at, :], tap_sems.at[n]))
    for n, (parity, ref) in enumerate(((core, val_ref), (1 - core, val_got_ref))):
        for at in range(0, ref.shape[1], shard):
            cols = pl.ds(pl.multiple_of(2 * at + parity * shard, shard), shard)
            copies.append(
                pltpu.make_async_copy(
                    ref.at[:, pl.ds(at, shard)], val_hbm.at[:, cols], sems.at[n, at // shard]
                )
            )
    for copy in copies:
        copy.start()
    for copy in copies:
        copy.wait()


def place(me, taps_mine, taps_got, values, values_got, shard):
    rows, taps = taps_mine.shape
    positions, width = values.shape
    return pl.pallas_call(
        functools.partial(place_kernel, shard),
        in_specs=[SMEM_SPEC] + [VMEM_SPEC] * 4,
        out_specs=[HBM_SPEC] * 2,
        out_shape=[
            jax.ShapeDtypeStruct((positions, 2 * width), values.dtype),
            jax.ShapeDtypeStruct((2 * rows, taps), F32),
        ],
        scratch_shapes=[
            pltpu.SemaphoreType.DMA((2, width // shard)),
            pltpu.SemaphoreType.DMA((2,)),
        ],
        compiler_params=params(8),
        cost_estimate=cost(1, 4 * positions * width),
        name="place",
    )(me, taps_mine, taps_got, values, values_got)


def tap_grad_plain_kernel(cot_ref, after_ref, val_ref, wx_ref, wv_ref, wi_ref, o_ref):
    x = spectrum_of_window(wx_ref[...], cot_ref[...], after_ref[...])
    o_ref[...] = inverted(cross(x, spectrum_of_values(wv_ref[...], val_ref[...])), wi_ref[...])


def tap_grad_plain(cotangent, after, values, taps, tile):
    positions, channels = cotangent.shape
    wx, wv, _, wi, _ = transforms(positions, taps)
    data = pl.BlockSpec((positions, tile), lambda t: (0, t))
    whole = lambda w: pl.BlockSpec(w.shape, lambda t: (0, 0))
    return pl.pallas_call(
        tap_grad_plain_kernel,
        grid=(channels // tile,),
        in_specs=[data, data, data, whole(wx), whole(wv), whole(wi)],
        out_specs=pl.BlockSpec((taps, tile), lambda t: (0, t)),
        out_shape=jax.ShapeDtypeStruct((taps, channels), F32),
        name="tap_grad_plain",
    )(cotangent, after, values, wx, wv, wi)


def spectrum_of_filters(matrix, filters):
    return lax.dot_general(
        matrix,
        jnp.concatenate([filters, filters], axis=1),
        (((1,), (1,)), ((), ())),
        preferred_element_type=F32,
    )


def value_grad_kernel(pieces, me_ref, x_ref, *refs):
    next_refs = refs[:pieces]
    line_ref, line_y_ref, wf_ref, wi_ref, own_ref, other_ref = refs[pieces:]
    depth = line_ref.shape[0]
    me = me_ref[0]
    core0, row, at = me // 2 % 2 == 0, me // 4 % 2, me // 8
    for piece, next_ref in enumerate(next_refs):
        filters = []
        for z in range(piece * depth // pieces, (piece + 1) * depth // pieces):
            for y in range(2):
                filters.append(jnp.where(row == y, line_ref[z ^ at], line_y_ref[z ^ at]))
        spectrum = spectrum_of_filters(wf_ref[...], jnp.concatenate(filters, axis=0))
        width = next_ref.shape[1]
        cols = pl.ds(piece * width, width)
        first = inverted(cross(x_ref[:, cols], spectrum), wi_ref[...]).astype(BF16)
        second = inverted(cross(next_ref[...], spectrum), wi_ref[...]).astype(BF16)
        own_ref[:, cols] = jnp.where(core0, first, second)
        other_ref[:, cols] = jnp.where(core0, second, first)


def value_grad_pair(me, near, far, line, line_y, positions):
    _, _, wf, _, wi = transforms(positions, line.shape[-1])
    half = jax.ShapeDtypeStruct((positions, near.shape[1]), BF16)
    return pl.pallas_call(
        functools.partial(value_grad_kernel, len(far)),
        in_specs=[SMEM_SPEC] + [VMEM_SPEC] * (5 + len(far)),
        out_specs=[VMEM_SPEC] * 2,
        out_shape=[half] * 2,
        compiler_params=params(24),
        cost_estimate=cost(2 * 8 * 128 * 256 * near.shape[1], 24 * positions * near.shape[1]),
        name="value_grad_pair",
    )(me, near, *far, line, line_y, wf, wi)


def value_grad_plain_kernel(cot_ref, after_ref, f_ref, wx_ref, wf_ref, wi_ref, o_ref):
    x = spectrum_of_window(wx_ref[...], cot_ref[...], after_ref[...])
    product = cross(x, spectrum_of_filters(wf_ref[...], f_ref[...]))
    o_ref[...] = inverted(product, wi_ref[...]).astype(BF16)


def value_grad_plain(cotangent, after, filters, tile):
    positions, channels = cotangent.shape
    taps = filters.shape[1]
    wx, _, wf, _, wi = transforms(positions, taps)
    data = pl.BlockSpec((positions, tile), lambda t: (0, t))
    whole = lambda w: pl.BlockSpec(w.shape, lambda t: (0, 0))
    return pl.pallas_call(
        value_grad_plain_kernel,
        grid=(channels // tile,),
        in_specs=[data, data, pl.BlockSpec((tile, taps), lambda t: (t, 0)), whole(wx), whole(wf), whole(wi)],
        out_specs=data,
        out_shape=jax.ShapeDtypeStruct((positions, channels), BF16),
        name="value_grad_plain",
    )(cotangent, after, filters, wx, wf, wi)


def body(token_ids, queries, gated_values, out_grad, filters):
    queries, gated_values, out_grad = queries[0], gated_values[0], out_grad[0]
    positions, _ = queries.shape
    shard, taps = filters.shape
    seqs, parts = lax.axis_size("dp"), lax.axis_size("ctx")
    factor = float(seqs * parts * positions) ** -0.5

    staged = (
        seqs == 2
        and parts >= 8
        and parts & (parts - 1) == 0
        and shard == 2 * LANES
        and positions == taps == LANES
    )
    if not staged:
        (cotangent,) = cotangent_of(token_ids, queries, out_grad, 1)
        after = lax.ppermute(cotangent, "ctx", [(i, i - 1) for i in range(1, parts)])
        all_filters = lax.all_gather(filters, "ctx", axis=0, tiled=True)
        value_grad = value_grad_plain(cotangent, after, all_filters, 512)
        share = tap_grad_plain(cotangent, after, gated_values, taps, 512)
        share = lax.psum_scatter(share.T * factor, "ctx", scatter_dimension=0, tiled=True)
        return value_grad[None], lax.psum(share, "dp")

    devices = seqs * parts
    depth = parts // 4
    pieces = 2
    rank = lax.axis_index("dp")
    part = lax.axis_index("ctx")
    me = (part * 2 + rank).astype(jnp.int32).reshape(1)

    def swap(x, bits):
        return lax.ppermute(x, AXES, [(i, i ^ bits) for i in range(devices)])

    def to_previous_chip(x, core):
        pairs = [
            (seq * parts + i, seq * parts + i - 2 + core)
            for seq in range(seqs)
            for i in range(2, parts, 2)
        ]
        return lax.ppermute(x, AXES, pairs)

    hops = (parts, 2, parts + 2)
    line = [filters] + [swap(filters, 4 * k) for k in range(1, depth)]

    *halos, own, other = cotangent_pair(me, token_ids, queries, out_grad, pieces, shard)
    afters = [
        [to_previous_chip(halos[2 * i + core], core) for core in range(2)]
        for i in range(pieces)
    ]
    got = swap(other, 1)
    values, other = split(me, gated_values, shard)
    values_got = swap(other, 1)
    near, product, v = near_window(me, own, got, values, values_got, taps)

    sums, far = [], []
    for i in range(pieces):
        mine, *sends, x = tap_grad(me, own, got, afters[i], product, v, i, taps)
        sums.append([mine] + [swap(x, bits) for x, bits in zip(sends, hops)])
        far.append(x)

    line = collect(line)
    line_y = swap(line, 2)
    grad, other = value_grad_pair(me, near, far, line, line_y, positions)
    grad_got = swap(other, 1)

    block, *sends = along_line(me, sums)
    block = finish(block, [swap(x, 4 * k) for k, x in enumerate(sends, 1)], factor)
    value_grad, filter_grad = place(me, block, swap(block, parts), grad, grad_got, shard)
    return value_grad[None], filter_grad


def solution(mesh):
    return jax.shard_map(
        body,
        mesh=mesh,
        in_specs=(
            P("dp", "ctx"),
            P("dp", "ctx", None),
            P("dp", "ctx", None),
            P("dp", "ctx", None),
            P("ctx", None),
        ),
        out_specs=(P("dp", "ctx", None), P("ctx", None)),
        check_vma=False,
    )
```

```python
import functools

import jax
import jax.numpy as jnp
import numpy as np
from jax import lax
from jax.experimental import pallas as pl
from jax.experimental.pallas import tpu as pltpu
from jax.sharding import PartitionSpec as P


BF16 = jnp.bfloat16
F32 = jnp.float32
AXES = ("dp", "ctx")
LANES = 128


def split_bf16(matrix):
    high = matrix.astype(BF16)
    low = (matrix - high.astype(np.float64)).astype(BF16)
    return np.asarray(high), np.asarray(low)


@functools.lru_cache(None)
def transforms(positions, taps):
    window = positions + taps
    half = window // 2
    angle = 2.0 * np.pi * np.outer(np.arange(half) + 0.5, np.arange(window)) / window
    forward = np.concatenate([np.cos(angle), np.sin(angle)], axis=0)
    high, low = split_bf16(forward)
    of_window = np.concatenate([high, low], axis=0)
    of_values = np.concatenate([high[:, :positions], low[:, :positions]], axis=1)
    of_taps = np.concatenate([high[:, :taps], low[:, :taps]], axis=1)
    inverse = forward.T / half
    inv_high, inv_low = split_bf16(inverse)
    to_taps = np.concatenate([inv_high[:taps], inv_low[:taps]], axis=0)
    to_positions = np.concatenate([inv_high[:positions], inv_low[:positions]], axis=0)
    return of_window, of_values, of_taps, to_taps, to_positions


def mul(a, b):
    return jnp.dot(a, b, preferred_element_type=F32)


def spectrum_of_window(matrix, own, after):
    both = mul(matrix, jnp.concatenate([own, after], axis=0))
    rows = both.shape[0] // 2
    return both[:rows] + both[rows:]


def cross(x, y):
    half = x.shape[0] // 2
    a, b, c, d = x[:half], x[half:], y[:half], y[half:]
    return jnp.concatenate([a * c + b * d, b * c - a * d], axis=0)


def inverted(product, inverse):
    high = product.astype(BF16)
    low = (product - high.astype(F32)).astype(BF16)
    rows = inverse.shape[0] // 2
    both = mul(inverse, high)
    return both[:rows] + both[rows:] + mul(inverse[:rows], low)


def spectrum_of_values(matrix, values):
    return mul(matrix, jnp.concatenate([values, values], axis=0))


VMEM_SPEC = pl.BlockSpec(memory_space=pltpu.VMEM)
SMEM_SPEC = pl.BlockSpec(memory_space=pltpu.SMEM)
HBM_SPEC = pl.BlockSpec(memory_space=pltpu.HBM)


def params(mib):
    return pltpu.CompilerParams(vmem_limit_bytes=mib << 20)


def cost(flops, nbytes):
    return pl.CostEstimate(flops=flops, bytes_accessed=nbytes, transcendentals=0)


def cotangent_kernel(ids_hbm, q_hbm, g_hbm, *refs):
    *outs, ids_ref, q_ref, g_ref, sems, ids_sem = refs
    width = outs[0].shape[1]
    copies = []
    ids_copy = pltpu.make_async_copy(ids_hbm, ids_ref, ids_sem)
    ids_copy.start()
    for i in range(len(outs)):
        cols = pl.ds(i * width, width)
        copies.append(
            [
                pltpu.make_async_copy(src.at[:, cols], dst.at[:, cols], sems.at[n, i])
                for n, (src, dst) in enumerate(((q_hbm, q_ref), (g_hbm, g_ref)))
            ]
        )
        for copy in copies[-1]:
            copy.start()
    positions = ids_ref.shape[1]
    ids_copy.wait()
    weight = jnp.where(ids_ref[...] < 4, 1.0, 0.1).astype(F32)
    weight = jnp.broadcast_to(weight, (LANES, positions)).T
    for i, out in enumerate(outs):
        for copy in copies[i]:
            copy.wait()
        for at in range(0, width, LANES):
            cols = pl.ds(i * width + at, LANES)
            out[:, at : at + LANES] = (
                weight * g_ref[:, cols].astype(F32) * q_ref[:, cols].astype(F32)
            ).astype(BF16)


def cotangent_of(token_ids, queries, out_grad, pieces):
    positions, channels = queries.shape
    piece = jax.ShapeDtypeStruct((positions, channels // pieces), BF16)
    return pl.pallas_call(
        cotangent_kernel,
        in_specs=[HBM_SPEC] * 3,
        out_specs=[VMEM_SPEC] * pieces,
        out_shape=[piece] * pieces,
        scratch_shapes=[pltpu.VMEM(token_ids.shape, token_ids.dtype)]
        + [pltpu.VMEM((positions, channels), BF16)] * 2
        + [pltpu.SemaphoreType.DMA((2, pieces)), pltpu.SemaphoreType.DMA],
        compiler_params=params(8),
        cost_estimate=cost(2 * positions * channels, 6 * positions * channels),
        name="cotangent",
    )(*(pltpu.with_memory_space_constraint(x, pltpu.HBM) for x in (token_ids, queries, out_grad)))


def cotangent_pair_kernel(
    pieces, shard, me_ref, ids_hbm, q_hbm, g_hbm, own_ref, other_ref, ids_ref, q_ref, g_ref, sems, ids_sem
):
    core0 = me_ref[0] // 2 % 2 == 0
    width = q_ref.shape[1] // pieces
    copies = []
    ids_copy = pltpu.make_async_copy(ids_hbm, ids_ref, ids_sem)
    ids_copy.start()
    for i in range(pieces):
        cols = pl.ds(i * width, width)
        copies.append(
            [
                pltpu.make_async_copy(src.at[:, cols], dst.at[:, cols], sems.at[n, i])
                for n, (src, dst) in enumerate(((q_hbm, q_ref), (g_hbm, g_ref)))
            ]
        )
        for copy in copies[-1]:
            copy.start()
    positions = ids_ref.shape[1]
    ids_copy.wait()
    weight = jnp.where(ids_ref[...] < 4, 1.0, 0.1).astype(F32)
    weight = jnp.broadcast_to(weight, (LANES, positions)).T

    def cotangent(at):
        cols = pl.ds(at, LANES)
        return (weight * g_ref[:, cols].astype(F32) * q_ref[:, cols].astype(F32)).astype(BF16)

    for i in range(pieces):
        for copy in copies[i]:
            copy.wait()
        for at in range(0, width // 2, LANES):
            source = i * width + at // shard * 2 * shard + at % shard
            even, odd = cotangent(source), cotangent(source + shard)
            cols = pl.ds(i * width // 2 + at, LANES)
            own_ref[:, cols] = jnp.where(core0, even, odd)
            other_ref[:, cols] = jnp.where(core0, odd, even)


def cotangent_pair(me, token_ids, queries, out_grad, pieces, shard):
    positions, channels = queries.shape
    half = jax.ShapeDtypeStruct((positions, channels // 2), BF16)
    return pl.pallas_call(
        functools.partial(cotangent_pair_kernel, pieces, shard),
        in_specs=[SMEM_SPEC] + [HBM_SPEC] * 3,
        out_specs=[VMEM_SPEC] * 2,
        out_shape=[half] * 2,
        scratch_shapes=[pltpu.VMEM(token_ids.shape, token_ids.dtype)]
        + [pltpu.VMEM((positions, channels), BF16)] * 2
        + [pltpu.SemaphoreType.DMA((2, pieces)), pltpu.SemaphoreType.DMA],
        compiler_params=params(8),
        cost_estimate=cost(2 * positions * channels, 8 * positions * channels),
        name="cotangent_pair",
    )(me, *(pltpu.with_memory_space_constraint(x, pltpu.HBM) for x in (token_ids, queries, out_grad)))


def heads_kernel(me_ref, own_ref, got_ref, *head_refs):
    core0 = me_ref[0] // 2 % 2 == 0
    for i, ref in enumerate(head_refs):
        cols = pl.ds(i * ref.shape[1], ref.shape[1])
        ref[...] = jnp.where(core0, own_ref[:, cols], got_ref[:, cols])


def heads(me, own, got, pieces):
    positions, width = own.shape
    piece = jax.ShapeDtypeStruct((positions, width // pieces), own.dtype)
    return pl.pallas_call(
        heads_kernel,
        in_specs=[SMEM_SPEC] + [VMEM_SPEC] * 2,
        out_specs=[VMEM_SPEC] * pieces,
        out_shape=[piece] * pieces,
        compiler_params=params(8),
        cost_estimate=cost(1, 6 * positions * width),
        name="heads",
    )(me, own, got)


def split_kernel(shard, me_ref, src_hbm, own_ref, other_ref, sems):
    core = me_ref[0] // 2 % 2
    copies = []
    for n, (parity, ref) in enumerate(((core, own_ref), (1 - core, other_ref))):
        for at in range(0, own_ref.shape[1], shard):
            cols = pl.ds(pl.multiple_of(2 * at + parity * shard, shard), shard)
            copy = pltpu.make_async_copy(
                src_hbm.at[:, cols], ref.at[:, pl.ds(at, shard)], sems.at[n, at // shard]
            )
            copy.start()
            copies.append(copy)
    for copy in copies:
        copy.wait()


def split(me, values, shard):
    positions, channels = values.shape
    half = jax.ShapeDtypeStruct((positions, channels // 2), values.dtype)
    return pl.pallas_call(
        functools.partial(split_kernel, shard),
        in_specs=[SMEM_SPEC, HBM_SPEC],
        out_specs=[VMEM_SPEC] * 2,
        out_shape=[half] * 2,
        scratch_shapes=[pltpu.SemaphoreType.DMA((2, channels // 2 // shard))],
        compiler_params=params(8),
        cost_estimate=cost(1, 4 * positions * channels),
        name="split",
    )(me, pltpu.with_memory_space_constraint(values, pltpu.HBM))


def near_window_kernel(
    me_ref, own_ref, got_ref, val_ref, val_got_ref, wx_ref, wv_ref, x_ref, product_ref, v_ref
):
    core0 = me_ref[0] // 2 % 2 == 0
    own, got = own_ref[...], got_ref[...]
    x = spectrum_of_window(wx_ref[...], jnp.where(core0, own, got), jnp.where(core0, got, own))
    x_ref[...] = x
    own, got = val_ref[...], val_got_ref[...]
    v_ref[...] = spectrum_of_values(wv_ref[...], jnp.where(core0, got, own))
    product_ref[...] = cross(x, spectrum_of_values(wv_ref[...], jnp.where(core0, own, got)))


def near_window(me, own, got, values, values_got, taps):
    positions, width = own.shape
    wx, wv, _, _, _ = transforms(positions, taps)
    spectrum = jax.ShapeDtypeStruct((wx.shape[1], width), F32)
    return pl.pallas_call(
        near_window_kernel,
        in_specs=[SMEM_SPEC] + [VMEM_SPEC] * 6,
        out_specs=[VMEM_SPEC] * 3,
        out_shape=[spectrum] * 3,
        compiler_params=params(24),
        cost_estimate=cost(2 * 8 * 128 * 256 * width, 32 * positions * width),
        name="near_window",
    )(me, own, got, values, values_got, wx, wv)


def tap_grad_kernel(
    piece, me_ref, own_ref, got_ref, after_ref, product_ref, v_ref, wx_ref, wi_ref, *refs
):
    width = after_ref.shape[1]
    cols = pl.ds(piece * width, width)
    me = me_ref[0]
    core0, row, rank = me // 2 % 2 == 0, me // 4 % 2, me % 2
    own = jnp.where(core0, got_ref[:, cols], own_ref[:, cols])
    x = spectrum_of_window(wx_ref[...], own, after_ref[...])
    out = inverted(product_ref[:, cols] + cross(x, v_ref[:, cols]), wi_ref[...])
    if len(refs) == 2:
        out_ref, x_ref = refs
        out_ref[...], x_ref[...] = out, x
        return
    before_refs, (mine_ref, *send_refs, x_ref, tmp_ref) = refs[:piece], refs[piece:]
    x_ref[...] = x
    per_piece = width // LANES
    for block in range((piece + 1) * per_piece):
        half, y, z = block % 2, block // 2 % 2, block // 4
        at = block % per_piece * LANES
        source = before_refs[block // per_piece] if block < piece * per_piece else out
        tmp_ref[(half ^ rank) + 2 * (y ^ row), z] = source[:, at : at + LANES]
    mine_ref[...] = tmp_ref[0]
    for k, ref in enumerate(send_refs, 1):
        ref[...] = tmp_ref[k].astype(BF16)


def tap_grad(me, own, got, after, product, v, taps, piece, pieces, before):
    positions, width = after.shape
    wx, _, _, wi, _ = transforms(positions, taps)
    block = (pieces * width // (4 * LANES), taps, LANES)
    last = piece == pieces - 1
    out_shape = [jax.ShapeDtypeStruct((taps, width), F32)]
    if last:
        out_shape = [jax.ShapeDtypeStruct(block, F32)] + [jax.ShapeDtypeStruct(block, BF16)] * 3
    out_shape.append(jax.ShapeDtypeStruct((wx.shape[1], width), F32))
    before = list(before) if last else []
    return pl.pallas_call(
        functools.partial(tap_grad_kernel, piece),
        in_specs=[SMEM_SPEC] + [VMEM_SPEC] * (7 + len(before)),
        out_specs=[VMEM_SPEC] * len(out_shape),
        out_shape=out_shape,
        scratch_shapes=[pltpu.VMEM((4, *block), F32)] if last else [],
        compiler_params=params(24),
        cost_estimate=cost(2 * 7 * 128 * 256 * width, 24 * positions * width),
        name="tap_grad",
    )(me, own, got, after, product, v, wx, wi, *before)


def collect_kernel(*refs):
    *ins, out_ref = refs
    for i, ref in enumerate(ins):
        out_ref[i] = ref[...]


def collect(arrays):
    first = arrays[0]
    return pl.pallas_call(
        collect_kernel,
        in_specs=[VMEM_SPEC] * len(arrays),
        out_specs=VMEM_SPEC,
        out_shape=jax.ShapeDtypeStruct((len(arrays), *first.shape), first.dtype),
        compiler_params=params(8),
        cost_estimate=cost(1, 4 * len(arrays) * first.size),
        name="collect",
    )(*arrays)


def line_kernel(pieces, me_ref, *refs):
    ins, (mine_ref, *send_refs) = refs[: 4 * pieces], refs[4 * pieces : -1]
    sum_ref = refs[-1]
    depth = ins[0].shape[0]
    for piece in range(pieces):
        own, *got = ins[4 * piece : 4 * piece + 4]
        for z in range(depth):
            total = own[z]
            for ref in got:
                total = total + ref[z].astype(F32)
            sum_ref[piece * depth + z] = total
    at = me_ref[0] // 8
    mine_ref[...] = sum_ref[at]
    for k, send_ref in enumerate(send_refs, 1):
        send_ref[...] = sum_ref[at ^ k].astype(BF16)


def along_line(me, pieces):
    depth, taps, lanes = pieces[0][0].shape
    count = len(pieces) * depth
    flat = [array for piece in pieces for array in piece]
    return pl.pallas_call(
        functools.partial(line_kernel, len(pieces)),
        in_specs=[SMEM_SPEC] + [VMEM_SPEC] * len(flat),
        out_specs=[VMEM_SPEC] * count,
        out_shape=[jax.ShapeDtypeStruct((taps, lanes), F32)]
        + [jax.ShapeDtypeStruct((taps, lanes), BF16)] * (count - 1),
        scratch_shapes=[pltpu.VMEM((count, taps, lanes), F32)],
        compiler_params=params(8),
        cost_estimate=cost(4 * count * taps * lanes, 16 * count * taps * lanes),
        name="along_line",
    )(me, *flat)


def finish_kernel(factor, mine_ref, *refs):
    *got, out_ref = refs
    total = mine_ref[...]
    for ref in got:
        total = total + ref[...].astype(F32)
    out_ref[...] = (total * factor).T


def finish(mine, got, factor):
    taps, lanes = mine.shape
    return pl.pallas_call(
        functools.partial(finish_kernel, factor),
        in_specs=[VMEM_SPEC] * (1 + len(got)),
        out_specs=VMEM_SPEC,
        out_shape=jax.ShapeDtypeStruct((lanes, taps), F32),
        compiler_params=params(8),
        cost_estimate=cost(4 * taps * lanes, 16 * taps * lanes),
        name="finish",
    )(mine, *got)


def place_kernel(shard, me_ref, own_ref, got_ref, out_hbm, sems):
    core = me_ref[0] // 2 % 2
    copies = []
    for n, (parity, ref) in enumerate(((core, own_ref), (1 - core, got_ref))):
        for at in range(0, ref.shape[1], shard):
            cols = pl.ds(pl.multiple_of(2 * at + parity * shard, shard), shard)
            copy = pltpu.make_async_copy(
                ref.at[:, pl.ds(at, shard)], out_hbm.at[:, cols], sems.at[n, at // shard]
            )
            copy.start()
            copies.append(copy)
    for copy in copies:
        copy.wait()


def place(me, own, got, shard):
    positions, width = own.shape
    return pl.pallas_call(
        functools.partial(place_kernel, shard),
        in_specs=[SMEM_SPEC] + [VMEM_SPEC] * 2,
        out_specs=HBM_SPEC,
        out_shape=jax.ShapeDtypeStruct((positions, 2 * width), own.dtype),
        scratch_shapes=[pltpu.SemaphoreType.DMA((2, width // shard))],
        compiler_params=params(8),
        cost_estimate=cost(1, 8 * positions * width),
        name="place",
    )(me, own, got)


def join_kernel(me_ref, mine_ref, other_ref, out_hbm, sems):
    rank = me_ref[0] % 2
    rows = mine_ref.shape[0]
    copies = []
    for n, (half, ref) in enumerate(((rank, mine_ref), (1 - rank, other_ref))):
        at = pl.ds(pl.multiple_of(half * rows, rows), rows)
        copies.append(pltpu.make_async_copy(ref, out_hbm.at[at, :], sems.at[n]))
        copies[-1].start()
    for copy in copies:
        copy.wait()


def join(me, mine, other):
    rows, taps = mine.shape
    return pl.pallas_call(
        join_kernel,
        in_specs=[SMEM_SPEC] + [VMEM_SPEC] * 2,
        out_specs=HBM_SPEC,
        out_shape=jax.ShapeDtypeStruct((2 * rows, taps), F32),
        scratch_shapes=[pltpu.SemaphoreType.DMA((2,))],
        compiler_params=params(8),
        cost_estimate=cost(1, 16 * rows * taps),
        name="join",
    )(me, mine, other)


def tap_grad_plain_kernel(cot_ref, after_ref, val_ref, wx_ref, wv_ref, wi_ref, o_ref):
    x = spectrum_of_window(wx_ref[...], cot_ref[...], after_ref[...])
    o_ref[...] = inverted(cross(x, spectrum_of_values(wv_ref[...], val_ref[...])), wi_ref[...])


def tap_grad_plain(cotangent, after, values, taps, tile):
    positions, channels = cotangent.shape
    wx, wv, _, wi, _ = transforms(positions, taps)
    data = pl.BlockSpec((positions, tile), lambda t: (0, t))
    whole = lambda w: pl.BlockSpec(w.shape, lambda t: (0, 0))
    return pl.pallas_call(
        tap_grad_plain_kernel,
        grid=(channels // tile,),
        in_specs=[data, data, data, whole(wx), whole(wv), whole(wi)],
        out_specs=pl.BlockSpec((taps, tile), lambda t: (0, t)),
        out_shape=jax.ShapeDtypeStruct((taps, channels), F32),
        name="tap_grad_plain",
    )(cotangent, after, values, wx, wv, wi)


def spectrum_of_filters(matrix, filters):
    return lax.dot_general(
        matrix,
        jnp.concatenate([filters, filters], axis=1),
        (((1,), (1,)), ((), ())),
        preferred_element_type=F32,
    )


def value_grad_kernel(pieces, me_ref, x_ref, *refs):
    next_refs = refs[:pieces]
    filters_ref, wf_ref, wi_ref, own_ref, other_ref = refs[pieces:]
    depth = filters_ref.shape[0]
    me = me_ref[0]
    core0, row, at = me // 2 % 2 == 0, me // 4 % 2, me // 8
    for piece, next_ref in enumerate(next_refs):
        filters = []
        for z in range(piece * depth // pieces, (piece + 1) * depth // pieces):
            for y in range(2):
                filters.append(filters_ref[z ^ at, y ^ row])
        spectrum = spectrum_of_filters(wf_ref[...], jnp.concatenate(filters, axis=0))
        width = next_ref.shape[1]
        cols = pl.ds(piece * width, width)
        first = inverted(cross(x_ref[:, cols], spectrum), wi_ref[...]).astype(BF16)
        second = inverted(cross(next_ref[...], spectrum), wi_ref[...]).astype(BF16)
        own_ref[:, cols] = jnp.where(core0, first, second)
        other_ref[:, cols] = jnp.where(core0, second, first)


def value_grad_pair(me, near, far, filters, positions):
    _, _, wf, _, wi = transforms(positions, filters.shape[-1])
    half = jax.ShapeDtypeStruct((positions, near.shape[1]), BF16)
    return pl.pallas_call(
        functools.partial(value_grad_kernel, len(far)),
        in_specs=[SMEM_SPEC] + [VMEM_SPEC] * (4 + len(far)),
        out_specs=[VMEM_SPEC] * 2,
        out_shape=[half] * 2,
        compiler_params=params(24),
        cost_estimate=cost(2 * 8 * 128 * 256 * near.shape[1], 24 * positions * near.shape[1]),
        name="value_grad_pair",
    )(me, near, *far, filters, wf, wi)


def value_grad_plain_kernel(cot_ref, after_ref, f_ref, wx_ref, wf_ref, wi_ref, o_ref):
    x = spectrum_of_window(wx_ref[...], cot_ref[...], after_ref[...])
    product = cross(x, spectrum_of_filters(wf_ref[...], f_ref[...]))
    o_ref[...] = inverted(product, wi_ref[...]).astype(BF16)


def value_grad_plain(cotangent, after, filters, tile):
    positions, channels = cotangent.shape
    taps = filters.shape[1]
    wx, _, wf, _, wi = transforms(positions, taps)
    data = pl.BlockSpec((positions, tile), lambda t: (0, t))
    whole = lambda w: pl.BlockSpec(w.shape, lambda t: (0, 0))
    return pl.pallas_call(
        value_grad_plain_kernel,
        grid=(channels // tile,),
        in_specs=[data, data, pl.BlockSpec((tile, taps), lambda t: (t, 0)), whole(wx), whole(wf), whole(wi)],
        out_specs=data,
        out_shape=jax.ShapeDtypeStruct((positions, channels), BF16),
        name="value_grad_plain",
    )(cotangent, after, filters, wx, wf, wi)


def body(token_ids, queries, gated_values, out_grad, filters):
    queries, gated_values, out_grad = queries[0], gated_values[0], out_grad[0]
    positions, _ = queries.shape
    shard, taps = filters.shape
    seqs, parts = lax.axis_size("dp"), lax.axis_size("ctx")
    factor = float(seqs * parts * positions) ** -0.5

    staged = (
        seqs == 2
        and parts >= 8
        and parts & (parts - 1) == 0
        and shard == 2 * LANES
        and positions == taps == LANES
    )
    if not staged:
        (cotangent,) = cotangent_of(token_ids, queries, out_grad, 1)
        after = lax.ppermute(cotangent, "ctx", [(i, i - 1) for i in range(1, parts)])
        all_filters = lax.all_gather(filters, "ctx", axis=0, tiled=True)
        value_grad = value_grad_plain(cotangent, after, all_filters, 512)
        share = tap_grad_plain(cotangent, after, gated_values, taps, 512)
        share = lax.psum_scatter(share.T * factor, "ctx", scatter_dimension=0, tiled=True)
        return value_grad[None], lax.psum(share, "dp")

    devices = seqs * parts
    depth = parts // 4
    pieces = 2
    rank = lax.axis_index("dp")
    part = lax.axis_index("ctx")
    me = (part * 2 + rank).astype(jnp.int32).reshape(1)

    def swap(x, bits):
        return lax.ppermute(x, AXES, [(i, i ^ bits) for i in range(devices)])

    back = [(seq * parts + i, seq * parts + i - 2) for seq in range(seqs) for i in range(2, parts)]
    hops = (parts, 2, parts + 2)
    filters_y = swap(filters, 2)

    own, other = cotangent_pair(me, token_ids, queries, out_grad, 2 * pieces, shard)
    got = swap(other, 1)
    afters = []
    for head in heads(me, own, got, pieces):
        afters.append(lax.ppermute(head, AXES, back))
    values, other = split(me, gated_values, shard)
    values_got = swap(other, 1)
    near, product, v = near_window(me, own, got, values, values_got, taps)

    shares, far = [], []
    for i in range(pieces):
        *shares, x = tap_grad(
            me, own, got, afters[i], product, v, taps, i, pieces, shares
        )
        far.append(x)
    mine, *sends = shares
    sums = [[mine] + [swap(x, bits) for x, bits in zip(sends, hops)]]

    filters = collect([filters, filters_y])
    filters = [filters] + [swap(filters, 4 * k) for k in range(1, depth)]
    filters = collect(filters)
    grad, other = value_grad_pair(me, near, far, filters, positions)
    grad_got = swap(other, 1)

    block, *sends = along_line(me, sums)
    block = finish(block, [swap(x, 4 * k) for k, x in enumerate(sends, 1)], factor)
    value_grad = place(me, grad, grad_got, shard)
    filter_grad = join(me, block, swap(block, parts))
    return value_grad[None], filter_grad


def solution(mesh):
    return jax.shard_map(
        body,
        mesh=mesh,
        in_specs=(
            P("dp", "ctx"),
            P("dp", "ctx", None),
            P("dp", "ctx", None),
            P("dp", "ctx", None),
            P("ctx", None),
        ),
        out_specs=(P("dp", "ctx", None), P("ctx", None)),
        check_vma=False,
    )
```

```python
import functools

import jax
import jax.numpy as jnp
import numpy as np
from jax import lax
from jax.experimental import pallas as pl
from jax.experimental.pallas import tpu as pltpu
from jax.sharding import PartitionSpec as P


BF16 = jnp.bfloat16
F32 = jnp.float32
AXES = ("dp", "ctx")
LANES = 128


def split_bf16(matrix):
    high = matrix.astype(BF16)
    low = (matrix - high.astype(np.float64)).astype(BF16)
    return np.asarray(high), np.asarray(low)


@functools.lru_cache(None)
def transforms(positions, taps):
    window = positions + taps
    half = window // 2
    angle = 2.0 * np.pi * np.outer(np.arange(half) + 0.5, np.arange(window)) / window
    forward = np.concatenate([np.cos(angle), np.sin(angle)], axis=0)
    high, low = split_bf16(forward)
    of_window = np.concatenate([high, low], axis=0)
    of_values = np.concatenate([high[:, :positions], low[:, :positions]], axis=1)
    of_taps = np.concatenate([high[:, :taps], low[:, :taps]], axis=1)
    inverse = forward.T / half
    inv_high, inv_low = split_bf16(inverse)
    to_taps = np.concatenate([inv_high[:taps], inv_low[:taps]], axis=0)
    to_positions = np.concatenate([inv_high[:positions], inv_low[:positions]], axis=0)
    return of_window, of_values, of_taps, to_taps, to_positions


def mul(a, b):
    return jnp.dot(a, b, preferred_element_type=F32)


def spectrum_of_window(matrix, own, after):
    both = mul(matrix, jnp.concatenate([own, after], axis=0))
    rows = both.shape[0] // 2
    return both[:rows] + both[rows:]


def cross(x, y):
    half = x.shape[0] // 2
    a, b, c, d = x[:half], x[half:], y[:half], y[half:]
    return jnp.concatenate([a * c + b * d, b * c - a * d], axis=0)


def inverted(product, inverse):
    high = product.astype(BF16)
    low = (product - high.astype(F32)).astype(BF16)
    rows = inverse.shape[0] // 2
    both = mul(inverse, high)
    return both[:rows] + both[rows:] + mul(inverse[:rows], low)


def spectrum_of_values(matrix, values):
    return mul(matrix, jnp.concatenate([values, values], axis=0))


VMEM_SPEC = pl.BlockSpec(memory_space=pltpu.VMEM)
SMEM_SPEC = pl.BlockSpec(memory_space=pltpu.SMEM)
HBM_SPEC = pl.BlockSpec(memory_space=pltpu.HBM)


def params(mib):
    return pltpu.CompilerParams(vmem_limit_bytes=mib << 20)


def cost(flops, nbytes):
    return pl.CostEstimate(flops=flops, bytes_accessed=nbytes, transcendentals=0)


def cotangent_kernel(ids_hbm, q_hbm, g_hbm, *refs):
    *outs, ids_ref, q_ref, g_ref, sems, ids_sem = refs
    width = outs[0].shape[1]
    copies = []
    ids_copy = pltpu.make_async_copy(ids_hbm, ids_ref, ids_sem)
    ids_copy.start()
    for i in range(len(outs)):
        cols = pl.ds(i * width, width)
        copies.append(
            [
                pltpu.make_async_copy(src.at[:, cols], dst.at[:, cols], sems.at[n, i])
                for n, (src, dst) in enumerate(((q_hbm, q_ref), (g_hbm, g_ref)))
            ]
        )
        for copy in copies[-1]:
            copy.start()
    positions = ids_ref.shape[1]
    ids_copy.wait()
    weight = jnp.where(ids_ref[...] < 4, 1.0, 0.1).astype(F32)
    weight = jnp.broadcast_to(weight, (LANES, positions)).T
    for i, out in enumerate(outs):
        for copy in copies[i]:
            copy.wait()
        for at in range(0, width, LANES):
            cols = pl.ds(i * width + at, LANES)
            out[:, at : at + LANES] = (
                weight * g_ref[:, cols].astype(F32) * q_ref[:, cols].astype(F32)
            ).astype(BF16)


def cotangent_of(token_ids, queries, out_grad, pieces):
    positions, channels = queries.shape
    piece = jax.ShapeDtypeStruct((positions, channels // pieces), BF16)
    return pl.pallas_call(
        cotangent_kernel,
        in_specs=[HBM_SPEC] * 3,
        out_specs=[VMEM_SPEC] * pieces,
        out_shape=[piece] * pieces,
        scratch_shapes=[pltpu.VMEM(token_ids.shape, token_ids.dtype)]
        + [pltpu.VMEM((positions, channels), BF16)] * 2
        + [pltpu.SemaphoreType.DMA((2, pieces)), pltpu.SemaphoreType.DMA],
        compiler_params=params(8),
        cost_estimate=cost(2 * positions * channels, 6 * positions * channels),
        name="cotangent",
    )(*(pltpu.with_memory_space_constraint(x, pltpu.HBM) for x in (token_ids, queries, out_grad)))


def cotangent_pair_kernel(
    piece, cuts, shard, me_ref, ids_hbm, q_hbm, g_hbm, own_ref, other_ref, ids_ref, q_ref, g_ref, sems, ids_sem
):
    core0 = me_ref[0] // 2 % 2 == 0
    width = q_ref.shape[1]
    cut = width // cuts
    copies = []
    ids_copy = pltpu.make_async_copy(ids_hbm, ids_ref, ids_sem)
    ids_copy.start()
    for i in range(cuts):
        source, cols = pl.ds(piece * width + i * cut, cut), pl.ds(i * cut, cut)
        copies.append(
            [
                pltpu.make_async_copy(src.at[:, source], dst.at[:, cols], sems.at[n, i])
                for n, (src, dst) in enumerate(((q_hbm, q_ref), (g_hbm, g_ref)))
            ]
        )
        for copy in copies[-1]:
            copy.start()
    positions = ids_ref.shape[1]
    ids_copy.wait()
    weight = jnp.where(ids_ref[...] < 4, 1.0, 0.1).astype(F32)
    weight = jnp.broadcast_to(weight, (LANES, positions)).T

    def cotangent(at):
        cols = pl.ds(at, LANES)
        return (weight * g_ref[:, cols].astype(F32) * q_ref[:, cols].astype(F32)).astype(BF16)

    for i in range(cuts):
        for copy in copies[i]:
            copy.wait()
        for at in range(i * cut // 2, (i + 1) * cut // 2, LANES):
            source = at // shard * 2 * shard + at % shard
            even, odd = cotangent(source), cotangent(source + shard)
            cols = pl.ds(at, LANES)
            own_ref[:, cols] = jnp.where(core0, even, odd)
            other_ref[:, cols] = jnp.where(core0, odd, even)


def cotangent_pair(me, token_ids, queries, out_grad, piece, pieces, shard):
    positions, channels = queries.shape
    width = channels // pieces
    cuts = 2
    half = jax.ShapeDtypeStruct((positions, width // 2), BF16)
    return pl.pallas_call(
        functools.partial(cotangent_pair_kernel, piece, cuts, shard),
        in_specs=[SMEM_SPEC] + [HBM_SPEC] * 3,
        out_specs=[VMEM_SPEC] * 2,
        out_shape=[half] * 2,
        scratch_shapes=[pltpu.VMEM(token_ids.shape, token_ids.dtype)]
        + [pltpu.VMEM((positions, width), BF16)] * 2
        + [pltpu.SemaphoreType.DMA((2, cuts)), pltpu.SemaphoreType.DMA],
        compiler_params=params(8),
        cost_estimate=cost(2 * positions * width, 6 * positions * width),
        name="cotangent_pair",
    )(me, *(pltpu.with_memory_space_constraint(x, pltpu.HBM) for x in (token_ids, queries, out_grad)))


def head_kernel(me_ref, own_ref, got_ref, head_ref):
    head_ref[...] = jnp.where(me_ref[0] // 2 % 2 == 0, own_ref[...], got_ref[...])


def head(me, own, got):
    return pl.pallas_call(
        head_kernel,
        in_specs=[SMEM_SPEC] + [VMEM_SPEC] * 2,
        out_specs=VMEM_SPEC,
        out_shape=jax.ShapeDtypeStruct(own.shape, own.dtype),
        compiler_params=params(8),
        cost_estimate=cost(1, 6 * own.size),
        name="head",
    )(me, own, got)


def split_kernel(shard, me_ref, src_hbm, own_ref, other_ref, sems):
    core = me_ref[0] // 2 % 2
    copies = []
    for n, (parity, ref) in enumerate(((core, own_ref), (1 - core, other_ref))):
        for at in range(0, own_ref.shape[1], shard):
            cols = pl.ds(pl.multiple_of(2 * at + parity * shard, shard), shard)
            copy = pltpu.make_async_copy(
                src_hbm.at[:, cols], ref.at[:, pl.ds(at, shard)], sems.at[n, at // shard]
            )
            copy.start()
            copies.append(copy)
    for copy in copies:
        copy.wait()


def split(me, values, shard):
    positions, channels = values.shape
    half = jax.ShapeDtypeStruct((positions, channels // 2), values.dtype)
    return pl.pallas_call(
        functools.partial(split_kernel, shard),
        in_specs=[SMEM_SPEC, HBM_SPEC],
        out_specs=[VMEM_SPEC] * 2,
        out_shape=[half] * 2,
        scratch_shapes=[pltpu.SemaphoreType.DMA((2, channels // 2 // shard))],
        compiler_params=params(8),
        cost_estimate=cost(1, 4 * positions * channels),
        name="split",
    )(me, pltpu.with_memory_space_constraint(values, pltpu.HBM))


def near_window_kernel(
    pieces, me_ref, *refs
):
    owns, gots = refs[:pieces], refs[pieces : 2 * pieces]
    val_ref, val_got_ref, wx_ref, wv_ref, x_ref, product_ref, v_ref = refs[2 * pieces :]
    core0 = me_ref[0] // 2 % 2 == 0
    own, got = (jnp.concatenate([ref[...] for ref in refs], axis=1) for refs in (owns, gots))
    x = spectrum_of_window(wx_ref[...], jnp.where(core0, own, got), jnp.where(core0, got, own))
    x_ref[...] = x
    own, got = val_ref[...], val_got_ref[...]
    v_ref[...] = spectrum_of_values(wv_ref[...], jnp.where(core0, got, own))
    product_ref[...] = cross(x, spectrum_of_values(wv_ref[...], jnp.where(core0, own, got)))


def near_window(me, own, got, values, values_got, taps):
    positions, width = values.shape
    wx, wv, _, _, _ = transforms(positions, taps)
    spectrum = jax.ShapeDtypeStruct((wx.shape[1], width), F32)
    return pl.pallas_call(
        functools.partial(near_window_kernel, len(own)),
        in_specs=[SMEM_SPEC] + [VMEM_SPEC] * (2 * len(own) + 4),
        out_specs=[VMEM_SPEC] * 3,
        out_shape=[spectrum] * 3,
        compiler_params=params(24),
        cost_estimate=cost(2 * 8 * 128 * 256 * width, 32 * positions * width),
        name="near_window",
    )(me, *own, *got, values, values_got, wx, wv)


def tap_grad_kernel(
    piece, last_chip, me_ref, own_ref, got_ref, after_ref, product_ref, v_ref, wx_ref, wi_ref, *refs
):
    mine_ref, *send_refs, x_ref, tmp_ref = refs
    width = after_ref.shape[1]
    cols = pl.ds(piece * width, width)
    me = me_ref[0]
    core0, row, rank = me // 2 % 2 == 0, me // 4 % 2, me % 2
    own = jnp.where(core0, got_ref[...], own_ref[...])
    after = jnp.where(me // 4 == last_chip, 0.0, after_ref[...]).astype(BF16)
    x = spectrum_of_window(wx_ref[...], own, after)
    x_ref[...] = x
    out = inverted(product_ref[:, cols] + cross(x, v_ref[:, cols]), wi_ref[...])
    for block in range(width // LANES):
        half, y, z = block % 2, block // 2 % 2, block // 4
        tmp_ref[(half ^ rank) + 2 * (y ^ row), z] = out[:, block * LANES : (block + 1) * LANES]
    mine_ref[...] = tmp_ref[0]
    for k, ref in enumerate(send_refs, 1):
        ref[...] = tmp_ref[k].astype(BF16)


def tap_grad(me, own, got, after, product, v, taps, piece, last_chip):
    positions, width = after.shape
    wx, _, _, wi, _ = transforms(positions, taps)
    depth = width // (4 * LANES)
    block = (depth, taps, LANES)
    return pl.pallas_call(
        functools.partial(tap_grad_kernel, piece, last_chip),
        in_specs=[SMEM_SPEC] + [VMEM_SPEC] * 7,
        out_specs=[VMEM_SPEC] * 5,
        out_shape=[jax.ShapeDtypeStruct(block, F32)]
        + [jax.ShapeDtypeStruct(block, BF16)] * 3
        + [jax.ShapeDtypeStruct((wx.shape[1], width), F32)],
        scratch_shapes=[pltpu.VMEM((4, *block), F32)],
        compiler_params=params(24),
        cost_estimate=cost(2 * 7 * 128 * 256 * width, 24 * positions * width),
        name="tap_grad",
    )(me, own, got, after, product, v, wx, wi)


def collect_kernel(*refs):
    *ins, out_ref = refs
    for i, ref in enumerate(ins):
        out_ref[i] = ref[...]


def collect(arrays):
    first = arrays[0]
    return pl.pallas_call(
        collect_kernel,
        in_specs=[VMEM_SPEC] * len(arrays),
        out_specs=VMEM_SPEC,
        out_shape=jax.ShapeDtypeStruct((len(arrays), *first.shape), first.dtype),
        compiler_params=params(8),
        cost_estimate=cost(1, 4 * len(arrays) * first.size),
        name="collect",
    )(*arrays)


def line_kernel(pieces, me_ref, *refs):
    ins, (mine_ref, *send_refs) = refs[: 4 * pieces], refs[4 * pieces : -1]
    sum_ref = refs[-1]
    depth = ins[0].shape[0]
    for piece in range(pieces):
        own, *got = ins[4 * piece : 4 * piece + 4]
        for z in range(depth):
            total = own[z]
            for ref in got:
                total = total + ref[z].astype(F32)
            sum_ref[piece * depth + z] = total
    at = me_ref[0] // 8
    mine_ref[...] = sum_ref[at]
    for k, send_ref in enumerate(send_refs, 1):
        send_ref[...] = sum_ref[at ^ k].astype(BF16)


def along_line(me, pieces):
    depth, taps, lanes = pieces[0][0].shape
    count = len(pieces) * depth
    flat = [array for piece in pieces for array in piece]
    return pl.pallas_call(
        functools.partial(line_kernel, len(pieces)),
        in_specs=[SMEM_SPEC] + [VMEM_SPEC] * len(flat),
        out_specs=[VMEM_SPEC] * count,
        out_shape=[jax.ShapeDtypeStruct((taps, lanes), F32)]
        + [jax.ShapeDtypeStruct((taps, lanes), BF16)] * (count - 1),
        scratch_shapes=[pltpu.VMEM((count, taps, lanes), F32)],
        compiler_params=params(8),
        cost_estimate=cost(4 * count * taps * lanes, 16 * count * taps * lanes),
        name="along_line",
    )(me, *flat)


def finish_kernel(factor, mine_ref, *refs):
    *got, out_ref = refs
    total = mine_ref[...]
    for ref in got:
        total = total + ref[...].astype(F32)
    out_ref[...] = (total * factor).T


def finish(mine, got, factor):
    taps, lanes = mine.shape
    return pl.pallas_call(
        functools.partial(finish_kernel, factor),
        in_specs=[VMEM_SPEC] * (1 + len(got)),
        out_specs=VMEM_SPEC,
        out_shape=jax.ShapeDtypeStruct((lanes, taps), F32),
        compiler_params=params(8),
        cost_estimate=cost(4 * taps * lanes, 16 * taps * lanes),
        name="finish",
    )(mine, *got)


def place_kernel(shard, me_ref, own_ref, got_ref, out_hbm, sems):
    core = me_ref[0] // 2 % 2
    copies = []
    for n, (parity, ref) in enumerate(((core, own_ref), (1 - core, got_ref))):
        for at in range(0, ref.shape[1], shard):
            cols = pl.ds(pl.multiple_of(2 * at + parity * shard, shard), shard)
            copy = pltpu.make_async_copy(
                ref.at[:, pl.ds(at, shard)], out_hbm.at[:, cols], sems.at[n, at // shard]
            )
            copy.start()
            copies.append(copy)
    for copy in copies:
        copy.wait()


def place(me, own, got, shard):
    positions, width = own.shape
    return pl.pallas_call(
        functools.partial(place_kernel, shard),
        in_specs=[SMEM_SPEC] + [VMEM_SPEC] * 2,
        out_specs=HBM_SPEC,
        out_shape=jax.ShapeDtypeStruct((positions, 2 * width), own.dtype),
        scratch_shapes=[pltpu.SemaphoreType.DMA((2, width // shard))],
        compiler_params=params(8),
        cost_estimate=cost(1, 8 * positions * width),
        name="place",
    )(me, own, got)


def join_kernel(me_ref, mine_ref, other_ref, out_hbm, sems):
    rank = me_ref[0] % 2
    rows = mine_ref.shape[0]
    copies = []
    for n, (half, ref) in enumerate(((rank, mine_ref), (1 - rank, other_ref))):
        at = pl.ds(pl.multiple_of(half * rows, rows), rows)
        copies.append(pltpu.make_async_copy(ref, out_hbm.at[at, :], sems.at[n]))
        copies[-1].start()
    for copy in copies:
        copy.wait()


def join(me, mine, other):
    rows, taps = mine.shape
    return pl.pallas_call(
        join_kernel,
        in_specs=[SMEM_SPEC] + [VMEM_SPEC] * 2,
        out_specs=HBM_SPEC,
        out_shape=jax.ShapeDtypeStruct((2 * rows, taps), F32),
        scratch_shapes=[pltpu.SemaphoreType.DMA((2,))],
        compiler_params=params(8),
        cost_estimate=cost(1, 16 * rows * taps),
        name="join",
    )(me, mine, other)


def tap_grad_plain_kernel(cot_ref, after_ref, val_ref, wx_ref, wv_ref, wi_ref, o_ref):
    x = spectrum_of_window(wx_ref[...], cot_ref[...], after_ref[...])
    o_ref[...] = inverted(cross(x, spectrum_of_values(wv_ref[...], val_ref[...])), wi_ref[...])


def tap_grad_plain(cotangent, after, values, taps, tile):
    positions, channels = cotangent.shape
    wx, wv, _, wi, _ = transforms(positions, taps)
    data = pl.BlockSpec((positions, tile), lambda t: (0, t))
    whole = lambda w: pl.BlockSpec(w.shape, lambda t: (0, 0))
    return pl.pallas_call(
        tap_grad_plain_kernel,
        grid=(channels // tile,),
        in_specs=[data, data, data, whole(wx), whole(wv), whole(wi)],
        out_specs=pl.BlockSpec((taps, tile), lambda t: (0, t)),
        out_shape=jax.ShapeDtypeStruct((taps, channels), F32),
        name="tap_grad_plain",
    )(cotangent, after, values, wx, wv, wi)


def spectrum_of_filters(matrix, filters):
    return lax.dot_general(
        matrix,
        jnp.concatenate([filters, filters], axis=1),
        (((1,), (1,)), ((), ())),
        preferred_element_type=F32,
    )


def value_grad_kernel(pieces, me_ref, x_ref, *refs):
    next_refs = refs[:pieces]
    filters_ref, wf_ref, wi_ref, own_ref, other_ref = refs[pieces:]
    depth = filters_ref.shape[0]
    me = me_ref[0]
    core0, row, at = me // 2 % 2 == 0, me // 4 % 2, me // 8
    for piece, next_ref in enumerate(next_refs):
        filters = []
        for z in range(piece * depth // pieces, (piece + 1) * depth // pieces):
            for y in range(2):
                filters.append(filters_ref[z ^ at, y ^ row])
        spectrum = spectrum_of_filters(wf_ref[...], jnp.concatenate(filters, axis=0))
        width = next_ref.shape[1]
        cols = pl.ds(piece * width, width)
        first = inverted(cross(x_ref[:, cols], spectrum), wi_ref[...]).astype(BF16)
        second = inverted(cross(next_ref[...], spectrum), wi_ref[...]).astype(BF16)
        own_ref[:, cols] = jnp.where(core0, first, second)
        other_ref[:, cols] = jnp.where(core0, second, first)


def value_grad_pair(me, near, far, filters, positions):
    _, _, wf, _, wi = transforms(positions, filters.shape[-1])
    half = jax.ShapeDtypeStruct((positions, near.shape[1]), BF16)
    return pl.pallas_call(
        functools.partial(value_grad_kernel, len(far)),
        in_specs=[SMEM_SPEC] + [VMEM_SPEC] * (4 + len(far)),
        out_specs=[VMEM_SPEC] * 2,
        out_shape=[half] * 2,
        compiler_params=params(24),
        cost_estimate=cost(2 * 8 * 128 * 256 * near.shape[1], 24 * positions * near.shape[1]),
        name="value_grad_pair",
    )(me, near, *far, filters, wf, wi)


def value_grad_plain_kernel(cot_ref, after_ref, f_ref, wx_ref, wf_ref, wi_ref, o_ref):
    x = spectrum_of_window(wx_ref[...], cot_ref[...], after_ref[...])
    product = cross(x, spectrum_of_filters(wf_ref[...], f_ref[...]))
    o_ref[...] = inverted(product, wi_ref[...]).astype(BF16)


def value_grad_plain(cotangent, after, filters, tile):
    positions, channels = cotangent.shape
    taps = filters.shape[1]
    wx, _, wf, _, wi = transforms(positions, taps)
    data = pl.BlockSpec((positions, tile), lambda t: (0, t))
    whole = lambda w: pl.BlockSpec(w.shape, lambda t: (0, 0))
    return pl.pallas_call(
        value_grad_plain_kernel,
        grid=(channels // tile,),
        in_specs=[data, data, pl.BlockSpec((tile, taps), lambda t: (t, 0)), whole(wx), whole(wf), whole(wi)],
        out_specs=data,
        out_shape=jax.ShapeDtypeStruct((positions, channels), BF16),
        name="value_grad_plain",
    )(cotangent, after, filters, wx, wf, wi)


def body(token_ids, queries, gated_values, out_grad, filters):
    queries, gated_values, out_grad = queries[0], gated_values[0], out_grad[0]
    positions, _ = queries.shape
    shard, taps = filters.shape
    seqs, parts = lax.axis_size("dp"), lax.axis_size("ctx")
    factor = float(seqs * parts * positions) ** -0.5

    staged = (
        seqs == 2
        and parts >= 8
        and parts & (parts - 1) == 0
        and shard == 2 * LANES
        and positions == taps == LANES
    )
    if not staged:
        (cotangent,) = cotangent_of(token_ids, queries, out_grad, 1)
        after = lax.ppermute(cotangent, "ctx", [(i, i - 1) for i in range(1, parts)])
        all_filters = lax.all_gather(filters, "ctx", axis=0, tiled=True)
        value_grad = value_grad_plain(cotangent, after, all_filters, 512)
        share = tap_grad_plain(cotangent, after, gated_values, taps, 512)
        share = lax.psum_scatter(share.T * factor, "ctx", scatter_dimension=0, tiled=True)
        return value_grad[None], lax.psum(share, "dp")

    devices = seqs * parts
    depth = parts // 4
    pieces = 2
    rank = lax.axis_index("dp")
    part = lax.axis_index("ctx")
    me = (part * 2 + rank).astype(jnp.int32).reshape(1)

    def swap(x, bits):
        return lax.ppermute(x, AXES, [(i, i ^ bits) for i in range(devices)])

    back = [
        (seq * parts + i, seq * parts + (i - 2) % parts) for seq in range(seqs) for i in range(parts)
    ]
    back_open = [pair for pair in back if pair[1] % parts < parts - 2]
    last_chip = parts // 2 - 1
    hops = (parts, 2, parts + 2)
    filters_y = swap(filters, 2)

    own, got, afters = [], [], []
    for i in range(pieces):
        mine, other = cotangent_pair(me, token_ids, queries, out_grad, i, pieces, shard)
        own.append(mine)
        got.append(swap(other, 1))
    for i in range(pieces):
        first = head(me, own[i], got[i])
        afters.append(lax.ppermute(first, AXES, back_open if i else back))
    values, other = split(me, gated_values, shard)
    values_got = swap(other, 1)
    near, product, v = near_window(me, own, got, values, values_got, taps)

    sums, far = [], []
    for i in range(pieces):
        mine, *sends, x = tap_grad(me, own[i], got[i], afters[i], product, v, taps, i, last_chip)
        got_sends = [swap(x, hops[k]) for k, x in enumerate(sends)]
        sums.append([mine] + got_sends)
        far.append(x)

    filters = collect([filters, filters_y])
    filters = [filters] + [swap(filters, 4 * k) for k in range(1, depth)]
    filters = collect(filters)
    grad, other = value_grad_pair(me, near, far, filters, positions)
    grad_got = swap(other, 1)

    block, *sends = along_line(me, sums)
    block = finish(block, [swap(x, 4 * k) for k, x in enumerate(sends, 1)], factor)
    value_grad = place(me, grad, grad_got, shard)
    filter_grad = join(me, block, swap(block, parts))
    return value_grad[None], filter_grad


def solution(mesh):
    return jax.shard_map(
        body,
        mesh=mesh,
        in_specs=(
            P("dp", "ctx"),
            P("dp", "ctx", None),
            P("dp", "ctx", None),
            P("dp", "ctx", None),
            P("ctx", None),
        ),
        out_specs=(P("dp", "ctx", None), P("ctx", None)),
        check_vma=False,
    )
```

```python
import functools

import jax
import jax.numpy as jnp
import numpy as np
from jax import lax
from jax.experimental import pallas as pl
from jax.experimental.pallas import tpu as pltpu
from jax.sharding import PartitionSpec as P


BF16 = jnp.bfloat16
F32 = jnp.float32
AXES = ("dp", "ctx")
LANES = 128


def split_bf16(matrix):
    high = matrix.astype(BF16)
    low = (matrix - high.astype(np.float64)).astype(BF16)
    return np.asarray(high), np.asarray(low)


@functools.lru_cache(None)
def transforms(positions, taps):
    window = positions + taps
    half = window // 2
    angle = 2.0 * np.pi * np.outer(np.arange(half) + 0.5, np.arange(window)) / window
    forward = np.concatenate([np.cos(angle), np.sin(angle)], axis=0)
    high, low = split_bf16(forward)
    of_window = np.concatenate([high, low], axis=0)
    of_values = np.concatenate([high[:, :positions], low[:, :positions]], axis=1)
    of_taps = np.concatenate([high[:, :taps], low[:, :taps]], axis=1)
    inverse = forward.T / half
    inv_high, inv_low = split_bf16(inverse)
    to_taps = np.concatenate([inv_high[:taps], inv_low[:taps]], axis=0)
    to_positions = np.concatenate([inv_high[:positions], inv_low[:positions]], axis=0)
    return of_window, of_values, of_taps, to_taps, to_positions


def mul(a, b):
    return jnp.dot(a, b, preferred_element_type=F32)


def spectrum_of_window(matrix, own, after):
    both = mul(matrix, jnp.concatenate([own, after], axis=0))
    rows = both.shape[0] // 2
    return both[:rows] + both[rows:]


def cross(x, y):
    half = x.shape[0] // 2
    a, b, c, d = x[:half], x[half:], y[:half], y[half:]
    return jnp.concatenate([a * c + b * d, b * c - a * d], axis=0)


def inverted(product, inverse):
    high = product.astype(BF16)
    low = (product - high.astype(F32)).astype(BF16)
    rows = inverse.shape[0] // 2
    both = mul(inverse, high)
    return both[:rows] + both[rows:] + mul(inverse[:rows], low)


def spectrum_of_values(matrix, values):
    return mul(matrix, jnp.concatenate([values, values], axis=0))


VMEM_SPEC = pl.BlockSpec(memory_space=pltpu.VMEM)
SMEM_SPEC = pl.BlockSpec(memory_space=pltpu.SMEM)
HBM_SPEC = pl.BlockSpec(memory_space=pltpu.HBM)


def params(mib):
    return pltpu.CompilerParams(vmem_limit_bytes=mib << 20)


def cost(flops, nbytes):
    return pl.CostEstimate(flops=flops, bytes_accessed=nbytes, transcendentals=0)


def cotangent_kernel(ids_hbm, q_hbm, g_hbm, *refs):
    *outs, ids_ref, q_ref, g_ref, sems, ids_sem = refs
    width = outs[0].shape[1]
    copies = []
    ids_copy = pltpu.make_async_copy(ids_hbm, ids_ref, ids_sem)
    ids_copy.start()
    for i in range(len(outs)):
        cols = pl.ds(i * width, width)
        copies.append(
            [
                pltpu.make_async_copy(src.at[:, cols], dst.at[:, cols], sems.at[n, i])
                for n, (src, dst) in enumerate(((q_hbm, q_ref), (g_hbm, g_ref)))
            ]
        )
        for copy in copies[-1]:
            copy.start()
    positions = ids_ref.shape[1]
    ids_copy.wait()
    weight = jnp.where(ids_ref[...] < 4, 1.0, 0.1).astype(F32)
    weight = jnp.broadcast_to(weight, (LANES, positions)).T
    for i, out in enumerate(outs):
        for copy in copies[i]:
            copy.wait()
        for at in range(0, width, LANES):
            cols = pl.ds(i * width + at, LANES)
            out[:, at : at + LANES] = (
                weight * g_ref[:, cols].astype(F32) * q_ref[:, cols].astype(F32)
            ).astype(BF16)


def cotangent_of(token_ids, queries, out_grad, pieces):
    positions, channels = queries.shape
    piece = jax.ShapeDtypeStruct((positions, channels // pieces), BF16)
    return pl.pallas_call(
        cotangent_kernel,
        in_specs=[HBM_SPEC] * 3,
        out_specs=[VMEM_SPEC] * pieces,
        out_shape=[piece] * pieces,
        scratch_shapes=[pltpu.VMEM(token_ids.shape, token_ids.dtype)]
        + [pltpu.VMEM((positions, channels), BF16)] * 2
        + [pltpu.SemaphoreType.DMA((2, pieces)), pltpu.SemaphoreType.DMA],
        compiler_params=params(8),
        cost_estimate=cost(2 * positions * channels, 6 * positions * channels),
        name="cotangent",
    )(*(pltpu.with_memory_space_constraint(x, pltpu.HBM) for x in (token_ids, queries, out_grad)))


def cotangent_pair_kernel(
    piece, cuts, shard, me_ref, ids_hbm, q_hbm, g_hbm, own_ref, other_ref, ids_ref, q_ref, g_ref, sems, ids_sem
):
    core0 = me_ref[0] // 2 % 2 == 0
    width = q_ref.shape[1]
    cut = width // cuts
    copies = []
    ids_copy = pltpu.make_async_copy(ids_hbm, ids_ref, ids_sem)
    ids_copy.start()
    for i in range(cuts):
        source, cols = pl.ds(piece * width + i * cut, cut), pl.ds(i * cut, cut)
        copies.append(
            [
                pltpu.make_async_copy(src.at[:, source], dst.at[:, cols], sems.at[n, i])
                for n, (src, dst) in enumerate(((q_hbm, q_ref), (g_hbm, g_ref)))
            ]
        )
        for copy in copies[-1]:
            copy.start()
    positions = ids_ref.shape[1]
    ids_copy.wait()
    weight = jnp.where(ids_ref[...] < 4, 1.0, 0.1).astype(F32)
    weight = jnp.broadcast_to(weight, (LANES, positions)).T

    def cotangent(at):
        cols = pl.ds(at, LANES)
        return (weight * g_ref[:, cols].astype(F32) * q_ref[:, cols].astype(F32)).astype(BF16)

    for i in range(cuts):
        for copy in copies[i]:
            copy.wait()
        for at in range(i * cut // 2, (i + 1) * cut // 2, LANES):
            source = at // shard * 2 * shard + at % shard
            even, odd = cotangent(source), cotangent(source + shard)
            cols = pl.ds(at, LANES)
            own_ref[:, cols] = jnp.where(core0, even, odd)
            other_ref[:, cols] = jnp.where(core0, odd, even)


def cotangent_pair(me, token_ids, queries, out_grad, piece, pieces, shard):
    positions, channels = queries.shape
    width = channels // pieces
    cuts = 2
    half = jax.ShapeDtypeStruct((positions, width // 2), BF16)
    return pl.pallas_call(
        functools.partial(cotangent_pair_kernel, piece, cuts, shard),
        in_specs=[SMEM_SPEC] + [HBM_SPEC] * 3,
        out_specs=[VMEM_SPEC] * 2,
        out_shape=[half] * 2,
        scratch_shapes=[pltpu.VMEM(token_ids.shape, token_ids.dtype)]
        + [pltpu.VMEM((positions, width), BF16)] * 2
        + [pltpu.SemaphoreType.DMA((2, cuts)), pltpu.SemaphoreType.DMA],
        compiler_params=params(8),
        cost_estimate=cost(2 * positions * width, 6 * positions * width),
        name="cotangent_pair",
    )(me, *(pltpu.with_memory_space_constraint(x, pltpu.HBM) for x in (token_ids, queries, out_grad)))


def head_kernel(me_ref, own_ref, got_ref, head_ref):
    head_ref[...] = jnp.where(me_ref[0] // 2 % 2 == 0, own_ref[...], got_ref[...])


def head(me, own, got):
    return pl.pallas_call(
        head_kernel,
        in_specs=[SMEM_SPEC] + [VMEM_SPEC] * 2,
        out_specs=VMEM_SPEC,
        out_shape=jax.ShapeDtypeStruct(own.shape, own.dtype),
        compiler_params=params(8),
        cost_estimate=cost(1, 6 * own.size),
        name="head",
    )(me, own, got)


def near_window_kernel(pieces, shard, me_ref, *refs):
    owns, gots = refs[:pieces], refs[pieces : 2 * pieces]
    val_ref, val_got_ref, wx_ref, wv_ref, x_ref, product_ref, v_ref = refs[2 * pieces :]
    core = me_ref[0] // 2 % 2
    core0 = core == 0
    own, got = (jnp.concatenate([ref[...] for ref in refs], axis=1) for refs in (owns, gots))
    x = spectrum_of_window(wx_ref[...], jnp.where(core0, own, got), jnp.where(core0, got, own))
    x_ref[...] = x
    own, got = (
        jnp.concatenate(
            [
                ref[:, pl.ds(pl.multiple_of(at + core * shard, shard), shard)]
                for at in range(0, ref.shape[1], 2 * shard)
            ],
            axis=1,
        )
        for ref in (val_ref, val_got_ref)
    )
    v_ref[...] = spectrum_of_values(wv_ref[...], jnp.where(core0, got, own))
    product_ref[...] = cross(x, spectrum_of_values(wv_ref[...], jnp.where(core0, own, got)))


def near_window(me, own, got, values, values_got, shard, taps):
    positions, width = values.shape[0], values.shape[1] // 2
    wx, wv, _, _, _ = transforms(positions, taps)
    spectrum = jax.ShapeDtypeStruct((wx.shape[1], width), F32)
    return pl.pallas_call(
        functools.partial(near_window_kernel, len(own), shard),
        in_specs=[SMEM_SPEC] + [VMEM_SPEC] * (2 * len(own) + 4),
        out_specs=[VMEM_SPEC] * 3,
        out_shape=[spectrum] * 3,
        compiler_params=params(24),
        cost_estimate=cost(2 * 8 * 128 * 256 * width, 32 * positions * width),
        name="near_window",
    )(me, *own, *got, values, values_got, wx, wv)


def tap_grad_kernel(
    piece, last_chip, me_ref, own_ref, got_ref, after_ref, product_ref, v_ref, wx_ref, wi_ref, *refs
):
    mine_ref, *send_refs, x_ref, tmp_ref = refs
    width = after_ref.shape[1]
    cols = pl.ds(piece * width, width)
    me = me_ref[0]
    core0, row, rank = me // 2 % 2 == 0, me // 4 % 2, me % 2
    own = jnp.where(core0, got_ref[...], own_ref[...])
    after = jnp.where(me // 4 == last_chip, 0.0, after_ref[...]).astype(BF16)
    x = spectrum_of_window(wx_ref[...], own, after)
    x_ref[...] = x
    out = inverted(product_ref[:, cols] + cross(x, v_ref[:, cols]), wi_ref[...])
    for block in range(width // LANES):
        half, y, z = block % 2, block // 2 % 2, block // 4
        tmp_ref[(half ^ rank) + 2 * (y ^ row), z] = out[:, block * LANES : (block + 1) * LANES]
    mine_ref[...] = tmp_ref[0]
    for k, ref in enumerate(send_refs, 1):
        ref[...] = tmp_ref[k].astype(BF16)


def tap_grad(me, own, got, after, product, v, taps, piece, last_chip):
    positions, width = after.shape
    wx, _, _, wi, _ = transforms(positions, taps)
    depth = width // (4 * LANES)
    block = (depth, taps, LANES)
    return pl.pallas_call(
        functools.partial(tap_grad_kernel, piece, last_chip),
        in_specs=[SMEM_SPEC] + [VMEM_SPEC] * 7,
        out_specs=[VMEM_SPEC] * 5,
        out_shape=[jax.ShapeDtypeStruct(block, F32)]
        + [jax.ShapeDtypeStruct(block, BF16)] * 3
        + [jax.ShapeDtypeStruct((wx.shape[1], width), F32)],
        scratch_shapes=[pltpu.VMEM((4, *block), F32)],
        compiler_params=params(24),
        cost_estimate=cost(2 * 7 * 128 * 256 * width, 24 * positions * width),
        name="tap_grad",
    )(me, own, got, after, product, v, wx, wi)


def collect_kernel(*refs):
    *ins, out_ref = refs
    for i, ref in enumerate(ins):
        out_ref[i] = ref[...]


def collect(arrays):
    first = arrays[0]
    return pl.pallas_call(
        collect_kernel,
        in_specs=[VMEM_SPEC] * len(arrays),
        out_specs=VMEM_SPEC,
        out_shape=jax.ShapeDtypeStruct((len(arrays), *first.shape), first.dtype),
        compiler_params=params(8),
        cost_estimate=cost(1, 4 * len(arrays) * first.size),
        name="collect",
    )(*arrays)


def line_kernel(pieces, me_ref, *refs):
    ins, (mine_ref, *send_refs) = refs[: 4 * pieces], refs[4 * pieces : -1]
    sum_ref = refs[-1]
    depth = ins[0].shape[0]
    for piece in range(pieces):
        own, *got = ins[4 * piece : 4 * piece + 4]
        for z in range(depth):
            total = own[z]
            for ref in got:
                total = total + ref[z].astype(F32)
            sum_ref[piece * depth + z] = total
    at = me_ref[0] // 8
    mine_ref[...] = sum_ref[at]
    for k, send_ref in enumerate(send_refs, 1):
        send_ref[...] = sum_ref[at ^ k].astype(BF16)


def along_line(me, pieces):
    depth, taps, lanes = pieces[0][0].shape
    count = len(pieces) * depth
    flat = [array for piece in pieces for array in piece]
    return pl.pallas_call(
        functools.partial(line_kernel, len(pieces)),
        in_specs=[SMEM_SPEC] + [VMEM_SPEC] * len(flat),
        out_specs=[VMEM_SPEC] * count,
        out_shape=[jax.ShapeDtypeStruct((taps, lanes), F32)]
        + [jax.ShapeDtypeStruct((taps, lanes), BF16)] * (count - 1),
        scratch_shapes=[pltpu.VMEM((count, taps, lanes), F32)],
        compiler_params=params(8),
        cost_estimate=cost(4 * count * taps * lanes, 16 * count * taps * lanes),
        name="along_line",
    )(me, *flat)


def finish_kernel(factor, mine_ref, *refs):
    *got, out_ref = refs
    total = mine_ref[...]
    for ref in got:
        total = total + ref[...].astype(F32)
    out_ref[...] = (total * factor).T


def finish(mine, got, factor):
    taps, lanes = mine.shape
    return pl.pallas_call(
        functools.partial(finish_kernel, factor),
        in_specs=[VMEM_SPEC] * (1 + len(got)),
        out_specs=VMEM_SPEC,
        out_shape=jax.ShapeDtypeStruct((lanes, taps), F32),
        compiler_params=params(8),
        cost_estimate=cost(4 * taps * lanes, 16 * taps * lanes),
        name="finish",
    )(mine, *got)


def place_kernel(shard, me_ref, own_ref, got_ref, out_hbm, sems):
    core = me_ref[0] // 2 % 2
    copies = []
    for n, (parity, ref) in enumerate(((core, own_ref), (1 - core, got_ref))):
        for at in range(0, ref.shape[1], shard):
            cols = pl.ds(pl.multiple_of(2 * at + parity * shard, shard), shard)
            copy = pltpu.make_async_copy(
                ref.at[:, pl.ds(at, shard)], out_hbm.at[:, cols], sems.at[n, at // shard]
            )
            copy.start()
            copies.append(copy)
    for copy in copies:
        copy.wait()


def place(me, own, got, shard):
    positions, width = own.shape
    return pl.pallas_call(
        functools.partial(place_kernel, shard),
        in_specs=[SMEM_SPEC] + [VMEM_SPEC] * 2,
        out_specs=HBM_SPEC,
        out_shape=jax.ShapeDtypeStruct((positions, 2 * width), own.dtype),
        scratch_shapes=[pltpu.SemaphoreType.DMA((2, width // shard))],
        compiler_params=params(8),
        cost_estimate=cost(1, 8 * positions * width),
        name="place",
    )(me, own, got)


def join_kernel(me_ref, mine_ref, other_ref, out_hbm, sems):
    rank = me_ref[0] % 2
    rows = mine_ref.shape[0]
    copies = []
    for n, (half, ref) in enumerate(((rank, mine_ref), (1 - rank, other_ref))):
        at = pl.ds(pl.multiple_of(half * rows, rows), rows)
        copies.append(pltpu.make_async_copy(ref, out_hbm.at[at, :], sems.at[n]))
        copies[-1].start()
    for copy in copies:
        copy.wait()


def join(me, mine, other):
    rows, taps = mine.shape
    return pl.pallas_call(
        join_kernel,
        in_specs=[SMEM_SPEC] + [VMEM_SPEC] * 2,
        out_specs=HBM_SPEC,
        out_shape=jax.ShapeDtypeStruct((2 * rows, taps), F32),
        scratch_shapes=[pltpu.SemaphoreType.DMA((2,))],
        compiler_params=params(8),
        cost_estimate=cost(1, 16 * rows * taps),
        name="join",
    )(me, mine, other)


def tap_grad_plain_kernel(cot_ref, after_ref, val_ref, wx_ref, wv_ref, wi_ref, o_ref):
    x = spectrum_of_window(wx_ref[...], cot_ref[...], after_ref[...])
    o_ref[...] = inverted(cross(x, spectrum_of_values(wv_ref[...], val_ref[...])), wi_ref[...])


def tap_grad_plain(cotangent, after, values, taps, tile):
    positions, channels = cotangent.shape
    wx, wv, _, wi, _ = transforms(positions, taps)
    data = pl.BlockSpec((positions, tile), lambda t: (0, t))
    whole = lambda w: pl.BlockSpec(w.shape, lambda t: (0, 0))
    return pl.pallas_call(
        tap_grad_plain_kernel,
        grid=(channels // tile,),
        in_specs=[data, data, data, whole(wx), whole(wv), whole(wi)],
        out_specs=pl.BlockSpec((taps, tile), lambda t: (0, t)),
        out_shape=jax.ShapeDtypeStruct((taps, channels), F32),
        name="tap_grad_plain",
    )(cotangent, after, values, wx, wv, wi)


def spectrum_of_filters(matrix, filters):
    return lax.dot_general(
        matrix,
        jnp.concatenate([filters, filters], axis=1),
        (((1,), (1,)), ((), ())),
        preferred_element_type=F32,
    )


def value_grad_kernel(pieces, me_ref, x_ref, *refs):
    next_refs = refs[:pieces]
    filters_ref, wf_ref, wi_ref, own_ref, other_ref = refs[pieces:]
    depth = filters_ref.shape[0]
    me = me_ref[0]
    core0, row, at = me // 2 % 2 == 0, me // 4 % 2, me // 8
    for piece, next_ref in enumerate(next_refs):
        filters = []
        for z in range(piece * depth // pieces, (piece + 1) * depth // pieces):
            for y in range(2):
                filters.append(filters_ref[z ^ at, y ^ row])
        spectrum = spectrum_of_filters(wf_ref[...], jnp.concatenate(filters, axis=0))
        width = next_ref.shape[1]
        cols = pl.ds(piece * width, width)
        first = inverted(cross(x_ref[:, cols], spectrum), wi_ref[...]).astype(BF16)
        second = inverted(cross(next_ref[...], spectrum), wi_ref[...]).astype(BF16)
        own_ref[:, cols] = jnp.where(core0, first, second)
        other_ref[:, cols] = jnp.where(core0, second, first)


def value_grad_pair(me, near, far, filters, positions):
    _, _, wf, _, wi = transforms(positions, filters.shape[-1])
    half = jax.ShapeDtypeStruct((positions, near.shape[1]), BF16)
    return pl.pallas_call(
        functools.partial(value_grad_kernel, len(far)),
        in_specs=[SMEM_SPEC] + [VMEM_SPEC] * (4 + len(far)),
        out_specs=[VMEM_SPEC] * 2,
        out_shape=[half] * 2,
        compiler_params=params(24),
        cost_estimate=cost(2 * 8 * 128 * 256 * near.shape[1], 24 * positions * near.shape[1]),
        name="value_grad_pair",
    )(me, near, *far, filters, wf, wi)


def value_grad_plain_kernel(cot_ref, after_ref, f_ref, wx_ref, wf_ref, wi_ref, o_ref):
    x = spectrum_of_window(wx_ref[...], cot_ref[...], after_ref[...])
    product = cross(x, spectrum_of_filters(wf_ref[...], f_ref[...]))
    o_ref[...] = inverted(product, wi_ref[...]).astype(BF16)


def value_grad_plain(cotangent, after, filters, tile):
    positions, channels = cotangent.shape
    taps = filters.shape[1]
    wx, _, wf, _, wi = transforms(positions, taps)
    data = pl.BlockSpec((positions, tile), lambda t: (0, t))
    whole = lambda w: pl.BlockSpec(w.shape, lambda t: (0, 0))
    return pl.pallas_call(
        value_grad_plain_kernel,
        grid=(channels // tile,),
        in_specs=[data, data, pl.BlockSpec((tile, taps), lambda t: (t, 0)), whole(wx), whole(wf), whole(wi)],
        out_specs=data,
        out_shape=jax.ShapeDtypeStruct((positions, channels), BF16),
        name="value_grad_plain",
    )(cotangent, after, filters, wx, wf, wi)


def body(token_ids, queries, gated_values, out_grad, filters):
    queries, gated_values, out_grad = queries[0], gated_values[0], out_grad[0]
    positions, _ = queries.shape
    shard, taps = filters.shape
    seqs, parts = lax.axis_size("dp"), lax.axis_size("ctx")
    factor = float(seqs * parts * positions) ** -0.5

    staged = (
        seqs == 2
        and parts >= 8
        and parts & (parts - 1) == 0
        and shard == 2 * LANES
        and positions == taps == LANES
    )
    if not staged:
        (cotangent,) = cotangent_of(token_ids, queries, out_grad, 1)
        after = lax.ppermute(cotangent, "ctx", [(i, i - 1) for i in range(1, parts)])
        all_filters = lax.all_gather(filters, "ctx", axis=0, tiled=True)
        value_grad = value_grad_plain(cotangent, after, all_filters, 512)
        share = tap_grad_plain(cotangent, after, gated_values, taps, 512)
        share = lax.psum_scatter(share.T * factor, "ctx", scatter_dimension=0, tiled=True)
        return value_grad[None], lax.psum(share, "dp")

    devices = seqs * parts
    depth = parts // 4
    pieces = 2
    rank = lax.axis_index("dp")
    part = lax.axis_index("ctx")
    me = (part * 2 + rank).astype(jnp.int32).reshape(1)

    def swap(x, bits):
        return lax.ppermute(x, AXES, [(i, i ^ bits) for i in range(devices)])

    back = [
        (seq * parts + i, seq * parts + (i - 2) % parts) for seq in range(seqs) for i in range(parts)
    ]
    back_open = [pair for pair in back if pair[1] % parts < parts - 2]
    last_chip = parts // 2 - 1
    hops = (parts, 2, parts + 2)
    filters_y = swap(filters, 2)

    own, got, afters = [], [], []
    for i in range(pieces):
        mine, other = cotangent_pair(me, token_ids, queries, out_grad, i, pieces, shard)
        own.append(mine)
        got.append(swap(other, 1))
    for i in range(pieces):
        first = head(me, own[i], got[i])
        afters.append(lax.ppermute(first, AXES, back_open if i else back))
    values_got = swap(gated_values, 1)
    near, product, v = near_window(
        me, own, got, gated_values, values_got, shard, taps
    )

    sums, far = [], []
    for i in range(pieces):
        mine, *sends, x = tap_grad(me, own[i], got[i], afters[i], product, v, taps, i, last_chip)
        got_sends = [swap(x, hops[k]) for k, x in enumerate(sends)]
        sums.append([mine] + got_sends)
        far.append(x)

    filters = collect([filters, filters_y])
    filters = [filters] + [swap(filters, 4 * k) for k in range(1, depth)]
    filters = collect(filters)
    grad, other = value_grad_pair(me, near, far, filters, positions)
    grad_got = swap(other, 1)

    block, *sends = along_line(me, sums)
    block = finish(block, [swap(x, 4 * k) for k, x in enumerate(sends, 1)], factor)
    value_grad = place(me, grad, grad_got, shard)
    filter_grad = join(me, block, swap(block, parts))
    return value_grad[None], filter_grad


def solution(mesh):
    return jax.shard_map(
        body,
        mesh=mesh,
        in_specs=(
            P("dp", "ctx"),
            P("dp", "ctx", None),
            P("dp", "ctx", None),
            P("dp", "ctx", None),
            P("ctx", None),
        ),
        out_specs=(P("dp", "ctx", None), P("ctx", None)),
        check_vma=False,
    )
```
